256 devices in a mesh: label: 8 (over x, core), dp: 8 (over z), basis: 4 (over y).
Axes of the slice: x: 4, y: 4, z: 8, core: 2. Of those that a mesh axis runs over, the one named last changes fastest.
Arguments:
- queries: bfloat16 [16384, 2048], P(('label', 'dp'), 'basis'), may hold values from -6 to 6
- basis: bfloat16 [256, 2048], P(None, 'basis'), may hold values from -0.125 to 0.125
- factors: bfloat16 [98304, 256], P('label'), may hold values from -0.375 to 0.375
- positives: int32 [16384, 16], P(('label', 'dp')), may hold values from 0 to 98303
- counts: int32 [16384], P(('label', 'dp')), may hold values from 1 to 16
- placement: int32 [98304], replicated, may hold values from 0 to 98303, each once
Outputs:
- grad_factors: float32 [98304, 256], P(('label', 'dp', 'basis'))
The draws below stay inside these ranges and needn't reach their ends.
Inputs may be any that keep to these rules, and one draw needn't show every extreme that they name: `placement`: each row number appears exactly once.
All inputs are finite; a program needn't handle non-finite values.
Results may differ from the reference program's by a relative error of at most 0.0012.
Values may be sent and summed in bfloat16 or wider, within the bound.
No kernel may reach another device: no remote copies, remote signals or barrier semaphores. Data moves between devices by JAX's collectives and lax.ppermute only.
A program may use at most 64 MiB of HBM per device.

```python
import math
import jax
import jax.numpy as jnp
import numpy as np
from jax import lax

R = 256
W = 2048
KP = 16
QUERIES = 16384
LABELS = 98304


def plant(array, own_key, smallest, largest):
    longest = array.shape.index(max(array.shape))
    spots = []
    for shift in (0, 1):
        where = [jax.random.randint(jax.random.fold_in(own_key, axis), (), 0, length) for axis, length in enumerate(array.shape)]
        where[longest] = (where[longest] + shift) % array.shape[longest]
        spots.append(tuple(where))
    return array.at[spots[0]].set(smallest).at[spots[1]].set(largest)


def block_levels(own_key, dims, cuts, smallest, largest):
    factor_of = 1.0
    for position, blocks in cuts:
        draws = jax.random.uniform(jax.random.fold_in(jax.random.fold_in(own_key, 6), position), (blocks,), jnp.float32, smallest / len(cuts), largest / len(cuts))
        factor_of = factor_of * jnp.repeat(jnp.exp(draws), dims[position] // blocks).reshape((-1,) + (1,) * (len(dims) - 1 - position))
    return factor_of


def wide_ids(key, shape, count, slope):
    loads = [min(1 << octave, count + 1 - (1 << octave)) * (1 << 20) // math.isqrt((1 << octave) ** slope) + 1 for octave in range((count + 1).bit_length()) if 1 << octave <= count]
    deviation = 1 + sum(loads) // (1 << 30)
    listing = np.cumsum(np.array([max(1, weight // deviation) for weight in loads]))
    lot = jax.random.randint(jax.random.fold_in(key, 1), shape, 0, int(listing[len(loads) - 1]))
    start = jnp.left_shift(1, jnp.searchsorted(jnp.asarray(listing, jnp.int32), lot, side="right").astype(jnp.int32))
    standing = start - 1 + jax.random.randint(jax.random.fold_in(key, 4), shape, 0, 1 << 30) % jnp.minimum(start, count + 1 - start)
    return jax.random.permutation(jax.random.fold_in(key, 2), count)[standing].astype(jnp.int32)


def scatter_about(key, shape, width, bound, shards=(), kind=jnp.bfloat16):
    values = jax.random.normal(key, shape, jnp.float32) * width
    if len(shards) > 0:
        values = block_levels(key, shape, shards, -0.22, 0.18) * values
    return jnp.clip(values, min=-bound, max=bound).astype(kind)


def setup_inputs(seed: int = 0) -> dict:
    keys = jax.random.split(jax.random.key(seed), 7)
    return {
        "queries": scatter_about(keys[0], (QUERIES, W), 1.0, 6.0, ((0, 64), (1, 4))),
        "basis": scatter_about(keys[1], (R, W), W ** -0.5, 0.125, ((1, 4),)),
        "factors": scatter_about(keys[2], (LABELS, R), R ** -0.5, 0.375, ((0, 8),)),
        "positives": plant(wide_ids(keys[3], (QUERIES, KP), LABELS, 2), jax.random.fold_in(keys[3], 3), 0, LABELS - 1).astype(jnp.int32),
        "counts": plant(jax.random.randint(keys[4], (QUERIES,), 1, KP + 1), jax.random.fold_in(keys[4], 1), 1, KP).astype(jnp.int32),
        "placement": jax.random.permutation(keys[5], LABELS).astype(jnp.int32),
    }


def reference(queries, basis, factors, positives, counts, placement):
    projected = jnp.dot(queries, basis.T, preferred_element_type=jnp.float32).astype(jnp.bfloat16)
    pos_rows = jnp.take(placement, positives, axis=0).astype(jnp.int32)
    slot_index = jnp.arange(KP, dtype=jnp.int32)
    pos_rows = jnp.where(slot_index[None, :] < counts[:, None], pos_rows, -1)
    weight = 1.0 / math.sqrt(QUERIES)
    label_step = math.gcd(LABELS, 2048)
    query_index = jnp.broadcast_to(jnp.arange(QUERIES, dtype=jnp.int32)[:, None], pos_rows.shape)

    def label_block(operand):
        factor_block, block_index = operand
        block_start = block_index * label_step
        local_rows = pos_rows - block_start
        inside = (local_rows >= 0) & (local_rows < label_step) & (pos_rows >= 0)
        target = jnp.zeros((QUERIES, label_step), jnp.float32).at[query_index, jnp.clip(local_rows, 0, label_step - 1)].max(inside.astype(jnp.float32))
        scores = jnp.dot(projected, factor_block.T, preferred_element_type=jnp.float32)
        logit_grad = (weight * (jax.nn.sigmoid(scores) - target)).astype(jnp.bfloat16)
        return jnp.dot(logit_grad.T, projected, preferred_element_type=jnp.float32)
    blocks = factors.reshape(LABELS // label_step, label_step, R)
    result = lax.map(label_block, (blocks, jnp.arange(LABELS // label_step, dtype=jnp.int32)))
    return result.reshape(LABELS, R)
```

```python
import functools

import jax
import jax.numpy as jnp
from jax import lax
from jax.experimental import pallas as pl
from jax.experimental.pallas import tpu as pltpu
from jax.sharding import PartitionSpec as P


SLOTS = 16
OWN = 64
EXTRA = 16
CHUNK = OWN + EXTRA
MIDDLE = 192
SCALE = 1.0 / 256.0
NOWHERE = -250.0


def digits_kernel(where_ref, pos_ref, counts_ref, place_ref, out_ref):
    shift, half = where_ref[0], where_ref[1]
    table = place_ref[...]
    high = ((table >> 8) - MIDDLE).astype(jnp.float32).astype(jnp.bfloat16)
    low = (table & 255).astype(jnp.float32).astype(jnp.bfloat16)
    tables = jnp.concatenate([high, low], axis=1)
    pos = pltpu.roll(pos_ref[...], shift, 1)[:, :128]
    counts = pltpu.roll(jnp.broadcast_to(counts_ref[...], (8, 256)), shift, 1)[0:1, :128]
    groups = table.shape[0]
    row = lax.broadcasted_iota(jnp.int32, (groups, 128), 0)
    lane = lax.broadcasted_iota(jnp.int32, (128, 128), 0)
    spot = lax.broadcasted_iota(jnp.int32, (1, 128), 1)
    mine = (spot >= half) & (spot < half + OWN)
    highs, lows = [], []
    for k in range(SLOTS):
        one = pos[k : k + 1, :]
        hot = jnp.where(row == (one >> 7), 1.0, 0.0).astype(jnp.bfloat16)
        both = lax.dot_general(tables, hot, (((0,), (0,)), ((), ())), preferred_element_type=jnp.float32)
        pick = lane == (one & 127)
        first = jnp.sum(jnp.where(pick, both[:128], 0.0), axis=0, keepdims=True)
        second = jnp.sum(jnp.where(pick, both[128:], 0.0), axis=0, keepdims=True)
        used = k < counts
        highs.append(jnp.where(mine, jnp.where(used, first, NOWHERE), 0.0))
        lows.append(jnp.where(mine & used, second, 0.0))
    out_ref[...] = jnp.concatenate(
        [jnp.concatenate(highs, axis=0), jnp.concatenate(lows, axis=0)], axis=1
    ).astype(jnp.bfloat16)


def grads_kernel(where_ref, factor_ref, payload_ref, *rest):
    outs, words_ref, acc_ref = rest[:-2], rest[-2], rest[-1]
    base, turn, flip = where_ref[0], where_ref[1], where_ref[2]
    labels = factor_ref.shape[0]
    word_count = labels // 32
    quarter = labels // len(outs)
    pairs = payload_ref.shape[0] // 2
    order = lax.broadcasted_iota(jnp.int32, (word_count, 128), 0) + turn
    order = jnp.where(order >= word_count, order - word_count, order)

    def build(p, carry):
        first = payload_ref[2 * p, OWN:CHUNK, :].astype(jnp.float32)
        second = payload_ref[2 * p + 1, OWN:CHUNK, :].astype(jnp.float32)
        both = (first + second).astype(jnp.int32)
        local = (both[:, :128] + MIDDLE) * 256 + both[:, 128:] - base
        local = pltpu.roll(local, flip, 1)
        word = local >> 5
        bit = jnp.left_shift(1, local & 31)
        found = jnp.zeros((word_count, 128), jnp.int32)
        for k in range(SLOTS):
            found = found | jnp.where(order == word[k : k + 1, :], bit[k : k + 1, :], 0)
        words_ref[p] = found
        return carry

    lax.fori_loop(0, pairs, build, 0)
    bits = jnp.left_shift(1, lax.broadcasted_iota(jnp.int32, (32, 128), 0))
    acc_ref[...] = jnp.zeros_like(acc_ref)

    def step(i, carry):
        proj = payload_ref[pl.ds(4 * i, 4), :OWN, :].reshape(4 * OWN, 256)
        scores = lax.dot_general(
            factor_ref[...], proj, (((1,), (1,)), ((), ())), preferred_element_type=jnp.float32
        )
        tanh = jnp.tanh(scores)
        columns = []
        for c in range(2):
            found = words_ref[2 * i + c]
            rows = []
            for m in range(word_count):
                hit = (jnp.broadcast_to(found[m : m + 1, :], (32, 128)) & bits) != 0
                piece = tanh[m * 32 : m * 32 + 32, c * 128 : c * 128 + 128]
                rows.append((piece + jnp.where(hit, -1.0, 1.0)).astype(jnp.bfloat16))
            columns.append(jnp.concatenate(rows, axis=0))
        grad = jnp.concatenate(columns, axis=1)
        acc_ref[...] += jnp.dot(grad, proj, preferred_element_type=jnp.float32)
        return carry

    lax.fori_loop(0, pairs // 2, step, 0)
    for j, out in enumerate(outs):
        out[...] = acc_ref[j * quarter : (j + 1) * quarter, :] * SCALE


def swap(value, axis, bit):
    size = lax.axis_size(axis)
    return lax.ppermute(value, axis, [(i, i ^ bit) for i in range(size)])


def shards(queries, basis, factors, positives, counts, placement):
    label, dp, part = lax.axis_index("label"), lax.axis_index("dp"), lax.axis_index("basis")
    parity = dp % 2
    partial_value = lax.dot_general(
        queries, basis, (((1,), (1,)), ((), ())), preferred_element_type=jnp.float32
    )

    vmem = pl.BlockSpec(memory_space=pltpu.VMEM)
    smem = pl.BlockSpec(memory_space=pltpu.SMEM)
    half = parity * OWN
    shift = (half - part * OWN) % 256
    digits = pl.pallas_call(
        digits_kernel,
        out_shape=jax.ShapeDtypeStruct((EXTRA, 256), jnp.bfloat16),
        in_specs=[smem, vmem, vmem, vmem],
        out_specs=vmem,
        cost_estimate=pl.CostEstimate(flops=1 << 30, bytes_accessed=1 << 19, transcendentals=0),
    )(
        jnp.stack([shift, half]).astype(jnp.int32),
        positives.T,
        counts.reshape(1, -1),
        placement.reshape(-1, 128),
    )

    block = factors.shape[0] // lax.axis_size("dp")
    quarter = block // lax.axis_size("basis")
    mine = lax.dynamic_slice_in_dim(factors, dp * block, block, 0)
    turned = jnp.concatenate([mine, mine], axis=0)
    turned = lax.dynamic_slice_in_dim(turned, part * quarter, block, 0) * jnp.bfloat16(0.5)

    rows = partial_value
    for bit in (2, 1):
        count = rows.shape[0] // 2
        high = (part // bit) % 2
        keep = lax.dynamic_slice_in_dim(rows, high * count, count, 0)
        send = lax.dynamic_slice_in_dim(rows, (1 - high) * count, count, 0)
        rows = keep + swap(send, "basis", bit)
    gathered = jnp.concatenate([rows.astype(jnp.bfloat16), digits], axis=0)[None]
    for axis, bit in (("dp", 1), ("dp", 4), ("dp", 2), ("label", 4), ("label", 2), ("label", 1)):
        gathered = jnp.concatenate([gathered, swap(gathered, axis, bit)], axis=0)

    where = jnp.stack(
        [label * factors.shape[0] + dp * block, part * (quarter // 32), half]
    ).astype(jnp.int32)
    outs = pl.pallas_call(
        grads_kernel,
        out_shape=[jax.ShapeDtypeStruct((quarter, 256), jnp.float32)] * 4,
        in_specs=[smem, vmem, vmem],
        out_specs=[vmem] * 4,
        scratch_shapes=[
            pltpu.VMEM((gathered.shape[0] // 2, block // 32, 128), jnp.int32),
            pltpu.VMEM((block, 256), jnp.float32),
        ],
        compiler_params=pltpu.CompilerParams(vmem_limit_bytes=48 * 1024 * 1024),
        cost_estimate=pl.CostEstimate(
            flops=1 << 33, bytes_accessed=1 << 22, transcendentals=1 << 22
        ),
    )(where, turned, gathered)
    total = outs[0]
    for step in (2, 1, 3):
        total = total + lax.ppermute(
            outs[step], "basis", [(i, (i + step) % 4) for i in range(4)]
        )
    return total


def solution(mesh):
    placed = (
        P(("label", "dp"), "basis"),
        P(None, "basis"),
        P("label", None),
        P(("label", "dp"), None),
        P(("label", "dp")),
        P(),
    )
    return jax.shard_map(
        shards,
        mesh=mesh,
        in_specs=placed,
        out_specs=P(("label", "dp", "basis"), None),
        check_vma=False,
    )
```

```python
import functools

import jax
import jax.numpy as jnp
from jax import lax
from jax.experimental import pallas as pl
from jax.experimental.pallas import tpu as pltpu
from jax.sharding import PartitionSpec as P


SLOTS = 16
OWN = 64
EXTRA = 16
CHUNK = OWN + EXTRA
MIDDLE = 192
SCALE = 1.0 / 256.0
NOWHERE = -250.0


def digits_kernel(where_ref, pos_ref, counts_ref, place_ref, out_ref):
    shift, half = where_ref[0], where_ref[1]
    table = place_ref[...]
    high = ((table >> 8) - MIDDLE).astype(jnp.float32).astype(jnp.bfloat16)
    low = (table & 255).astype(jnp.float32).astype(jnp.bfloat16)
    tables = jnp.concatenate([high, low], axis=1)
    pos = pltpu.roll(pos_ref[...], shift, 1)[:, :128]
    counts = pltpu.roll(jnp.broadcast_to(counts_ref[...], (8, 256)), shift, 1)[0:1, :128]
    groups = table.shape[0]
    row = lax.broadcasted_iota(jnp.int32, (groups, 128), 0)
    lane = lax.broadcasted_iota(jnp.int32, (128, 128), 0)
    spot = lax.broadcasted_iota(jnp.int32, (1, 128), 1)
    mine = (spot >= half) & (spot < half + OWN)
    highs, lows = [], []
    for k in range(SLOTS):
        one = pos[k : k + 1, :]
        hot = jnp.where(row == (one >> 7), 1.0, 0.0).astype(jnp.bfloat16)
        both = lax.dot_general(tables, hot, (((0,), (0,)), ((), ())), preferred_element_type=jnp.float32)
        pick = lane == (one & 127)
        first = jnp.sum(jnp.where(pick, both[:128], 0.0), axis=0, keepdims=True)
        second = jnp.sum(jnp.where(pick, both[128:], 0.0), axis=0, keepdims=True)
        used = k < counts
        highs.append(jnp.where(mine, jnp.where(used, first, NOWHERE), 0.0))
        lows.append(jnp.where(mine & used, second, 0.0))
    out_ref[...] = jnp.concatenate(
        [jnp.concatenate(highs, axis=0), jnp.concatenate(lows, axis=0)], axis=1
    ).astype(jnp.bfloat16)


def grads_kernel(first_call, where_ref, factor_ref, other_ref, payload_ref, *rest):
    if first_call:
        outs, words = rest[:2], rest[2:]
    else:
        olds, outs, words = rest[:2], rest[2:4], rest[4:]
    flip = where_ref[2]
    labels = factor_ref.shape[0]
    word_count = labels // 32
    pairs = payload_ref.shape[0] // 2
    order = lax.broadcasted_iota(jnp.int32, (word_count, 128), 0)

    def build(p, carry):
        first = payload_ref[2 * p, OWN:CHUNK, :].astype(jnp.float32)
        second = payload_ref[2 * p + 1, OWN:CHUNK, :].astype(jnp.float32)
        both = (first + second).astype(jnp.int32)
        rows = (both[:, :128] + MIDDLE) * 256 + both[:, 128:]
        rows = pltpu.roll(rows, flip, 1)
        for which in range(2):
            local = rows - where_ref[which]
            word = local >> 5
            bit = jnp.left_shift(1, local & 31)
            found = jnp.zeros((word_count, 128), jnp.int32)
            for k in range(SLOTS):
                found = found | jnp.where(order == word[k : k + 1, :], bit[k : k + 1, :], 0)
            words[which][p] = found
        return carry

    lax.fori_loop(0, pairs, build, 0)
    bits = jnp.left_shift(1, lax.broadcasted_iota(jnp.int32, (32, 128), 0))
    for which, factors in enumerate((factor_ref, other_ref)):
        out = outs[which]
        if first_call:
            out[...] = jnp.zeros_like(out)
        else:
            out[...] = olds[which][...]

        def step(i, carry, which=which, factors=factors, out=out):
            proj = payload_ref[pl.ds(4 * i, 4), :OWN, :].reshape(4 * OWN, 256)
            scores = lax.dot_general(
                factors[...],
                proj * jnp.bfloat16(0.5),
                (((1,), (1,)), ((), ())),
                preferred_element_type=jnp.float32,
            )
            tanh = jnp.tanh(scores)
            columns = []
            for c in range(2):
                found = words[which][2 * i + c]
                rows = []
                for m in range(word_count):
                    hit = (jnp.broadcast_to(found[m : m + 1, :], (32, 128)) & bits) != 0
                    piece = tanh[m * 32 : m * 32 + 32, c * 128 : c * 128 + 128]
                    rows.append((piece + jnp.where(hit, -1.0, 1.0)).astype(jnp.bfloat16))
                columns.append(jnp.concatenate(rows, axis=0))
            grad = jnp.concatenate(columns, axis=1)
            out[...] += jnp.dot(grad, proj, preferred_element_type=jnp.float32)
            return carry

        lax.fori_loop(0, pairs // 2, step, 0)


def join_kernel(*refs):
    out = refs[-1]
    spot = 0
    for ref in refs[:-1]:
        out[spot : spot + ref.shape[0]] = ref[...]
        spot += ref.shape[0]


VMEM = pl.BlockSpec(memory_space=pltpu.VMEM)
SMEM = pl.BlockSpec(memory_space=pltpu.SMEM)


def join(*pieces):
    count = sum(piece.shape[0] for piece in pieces)
    shape = jax.ShapeDtypeStruct((count,) + pieces[0].shape[1:], pieces[0].dtype)
    return pl.pallas_call(
        join_kernel, out_shape=shape, in_specs=[VMEM] * len(pieces), out_specs=VMEM
    )(*pieces)


def add_grads(where, factors, others, payload, sums=()):
    block = factors.shape[0]
    shape = jax.ShapeDtypeStruct((block, 256), jnp.float32)
    return pl.pallas_call(
        functools.partial(grads_kernel, not sums),
        out_shape=[shape, shape],
        in_specs=[SMEM] + [VMEM] * (3 + len(sums)),
        out_specs=[VMEM, VMEM],
        input_output_aliases={4: 0, 5: 1} if sums else {},
        scratch_shapes=[pltpu.VMEM((payload.shape[0] // 2, block // 32, 128), jnp.int32)] * 2,
        compiler_params=pltpu.CompilerParams(vmem_limit_bytes=32 * 1024 * 1024),
        cost_estimate=pl.CostEstimate(
            flops=8 * block * payload.shape[0] * OWN * 256,
            bytes_accessed=1 << 22,
            transcendentals=2 * block * payload.shape[0] * OWN,
        ),
    )(where, factors, others, payload, *sums)


def swap(value, axis, bit):
    size = lax.axis_size(axis)
    return lax.ppermute(value, axis, [(i, i ^ bit) for i in range(size)])


def shift_by(value, axis, step, inner=1):
    size = lax.axis_size(axis)
    return lax.ppermute(value, axis, [(i, (i + step * inner) % size) for i in range(size)])


def shards(queries, basis, factors, positives, counts, placement):
    label, dp, part = lax.axis_index("label"), lax.axis_index("dp"), lax.axis_index("basis")
    block = factors.shape[0] // lax.axis_size("dp")
    quarter = block // lax.axis_size("basis")
    half = (dp & 1) * OWN
    mine = lax.dynamic_slice_in_dim(factors, dp * block, block, 0)
    partial_value = lax.dot_general(
        queries, basis, (((1,), (1,)), ((), ())), preferred_element_type=jnp.float32
    )
    others = swap(mine, "label", 1)
    digits = pl.pallas_call(
        digits_kernel,
        out_shape=jax.ShapeDtypeStruct((EXTRA, 256), jnp.bfloat16),
        in_specs=[SMEM, VMEM, VMEM, VMEM],
        out_specs=VMEM,
        cost_estimate=pl.CostEstimate(flops=1 << 31, bytes_accessed=1 << 19, transcendentals=0),
    )(
        jnp.stack([(half - part * OWN) & 255, half]).astype(jnp.int32),
        positives.T,
        counts.reshape(1, -1),
        placement.reshape(-1, 128),
    )

    rows = partial_value
    for bit in (2, 1):
        count = rows.shape[0] // 2
        high = (part >> (bit - 1)) & 1
        keep = lax.dynamic_slice_in_dim(rows, high * count, count, 0)
        send = lax.dynamic_slice_in_dim(rows, (1 - high) * count, count, 0)
        rows = keep + swap(send, "basis", bit)
    own = jnp.concatenate([rows.astype(jnp.bfloat16), digits], axis=0)[None]
    pair = join(own, swap(own, "dp", 1))
    ring = join(pair, *(shift_by(pair, "dp", step) for step in (4, 2, 6)))

    first = label * factors.shape[0] + dp * block
    other = (label ^ 1) * factors.shape[0] + dp * block
    where = jnp.stack([first, other, half]).astype(jnp.int32)
    arrivals = [shift_by(ring, "label", step, 2) for step in (1, 3, 2)]
    sums = add_grads(where, mine, others, ring)
    for arrival in arrivals:
        sums = add_grads(where, mine, others, arrival, sums)
    total = sums[0] + swap(sums[1], "label", 1)

    def quarter_of(step):
        return lax.dynamic_slice_in_dim(total, ((part + step) & 3) * quarter, quarter, 0)

    far = quarter_of(2)
    up = shift_by(far[: quarter // 2], "basis", 1)
    down = shift_by(far[quarter // 2 :], "basis", 3)
    zeros = jnp.zeros_like(up)
    up = shift_by(quarter_of(1) + jnp.concatenate([up, zeros]), "basis", 1)
    down = shift_by(quarter_of(3) + jnp.concatenate([zeros, down]), "basis", 3)
    return (quarter_of(0) + up + down) * SCALE


def solution(mesh):
    placed = (
        P(("label", "dp"), "basis"),
        P(None, "basis"),
        P("label", None),
        P(("label", "dp"), None),
        P(("label", "dp")),
        P(),
    )
    return jax.shard_map(
        shards,
        mesh=mesh,
        in_specs=placed,
        out_specs=P(("label", "dp", "basis"), None),
        check_vma=False,
    )
```

```python
import functools

import jax
import jax.numpy as jnp
from jax import lax
from jax.experimental import pallas as pl
from jax.experimental.pallas import tpu as pltpu
from jax.sharding import PartitionSpec as P


SLOTS = 16
OWN = 64
EXTRA = 16
CHUNK = OWN + EXTRA
MIDDLE = 192
SCALE = 1.0 / 256.0
NOWHERE = -250.0


def digits_kernel(where_ref, pos_ref, counts_ref, place_ref, out_ref):
    shift, half = where_ref[0], where_ref[1]
    table = place_ref[...]
    high = ((table >> 8) - MIDDLE).astype(jnp.float32).astype(jnp.bfloat16)
    low = (table & 255).astype(jnp.float32).astype(jnp.bfloat16)
    tables = jnp.concatenate([high, low], axis=1)
    pos = pltpu.roll(pos_ref[...], shift, 1)[:, :128]
    counts = pltpu.roll(jnp.broadcast_to(counts_ref[...], (8, 256)), shift, 1)[0:1, :128]
    groups = table.shape[0]
    row = lax.broadcasted_iota(jnp.int32, (groups, 128), 0)
    lane = lax.broadcasted_iota(jnp.int32, (128, 128), 0)
    spot = lax.broadcasted_iota(jnp.int32, (1, 128), 1)
    mine = (spot >= half) & (spot < half + OWN)
    highs, lows = [], []
    for k in range(SLOTS):
        one = pos[k : k + 1, :]
        hot = jnp.where(row == (one >> 7), 1.0, 0.0).astype(jnp.bfloat16)
        both = lax.dot_general(tables, hot, (((0,), (0,)), ((), ())), preferred_element_type=jnp.float32)
        pick = lane == (one & 127)
        first = jnp.sum(jnp.where(pick, both[:128], 0.0), axis=0, keepdims=True)
        second = jnp.sum(jnp.where(pick, both[128:], 0.0), axis=0, keepdims=True)
        used = k < counts
        highs.append(jnp.where(mine, jnp.where(used, first, NOWHERE), 0.0))
        lows.append(jnp.where(mine & used, second, 0.0))
    out_ref[...] = jnp.concatenate(
        [jnp.concatenate(highs, axis=0), jnp.concatenate(lows, axis=0)], axis=1
    ).astype(jnp.bfloat16)


def build_words(which, base, flip, payload_refs, words_ref, word_ref, bit_ref):
    spot = 0
    for payload_ref in payload_refs:
        for p in range(payload_ref.shape[0] // 2):
            first = payload_ref[2 * p, OWN:CHUNK, :].astype(jnp.float32)
            second = payload_ref[2 * p + 1, OWN:CHUNK, :].astype(jnp.float32)
            both = (first + second).astype(jnp.int32)
            local = pltpu.roll((both[:, :128] + MIDDLE) * 256 + both[:, 128:], flip, 1) - base
            word_ref[spot] = local >> 5
            bit_ref[spot] = jnp.left_shift(1, local & 31)
            spot += 1
    shape = words_ref.shape[1:]
    order = lax.broadcasted_iota(jnp.int32, shape, 0)

    def build(p, carry):
        found = jnp.zeros(shape, jnp.int32)
        for k in range(SLOTS):
            word = jnp.broadcast_to(word_ref[p, k : k + 1, :], shape)
            bit = jnp.broadcast_to(bit_ref[p, k : k + 1, :], shape)
            found = found | jnp.where(order == word, bit, 0)
        words_ref[p] = found
        return carry

    lax.fori_loop(0, spot, build, 0)


def block_grads(factor_ref, payload_refs, words_ref):
    word_count = words_ref.shape[1]
    bits = jnp.left_shift(1, lax.broadcasted_iota(jnp.int32, (32, 128), 0))
    proj = [ref[:, :OWN, :].reshape(-1, 256) for ref in payload_refs]
    proj = proj[0] if len(proj) == 1 else jnp.concatenate(proj, axis=0)
    scores = lax.dot_general(
        factor_ref[...],
        proj * jnp.bfloat16(0.5),
        (((1,), (1,)), ((), ())),
        preferred_element_type=jnp.float32,
    )
    tanh = jnp.tanh(scores)
    columns = []
    for c in range(proj.shape[0] // 128):
        found = words_ref[c]
        rows = []
        for m in range(word_count):
            hit = (jnp.broadcast_to(found[m : m + 1, :], (32, 128)) & bits) != 0
            piece = tanh[m * 32 : m * 32 + 32, c * 128 : c * 128 + 128]
            rows.append((piece + jnp.where(hit, -1.0, 1.0)).astype(jnp.bfloat16))
        columns.append(jnp.concatenate(rows, axis=0))
    grad = jnp.concatenate(columns, axis=1)
    return jnp.dot(grad, proj, preferred_element_type=jnp.float32)


def grads_kernel(blocks, payloads, adds, where_ref, *refs):
    factors, refs = refs[: len(blocks)], refs[len(blocks) :]
    payload_refs, refs = refs[:payloads], refs[payloads:]
    olds, refs = refs[: len(blocks) * adds], refs[len(blocks) * adds :]
    outs, (words_ref, word_ref, bit_ref) = refs[: len(blocks)], refs[len(blocks) :]
    for i, which in enumerate(blocks):
        build_words(which, where_ref[which], where_ref[2], payload_refs, words_ref, word_ref, bit_ref)
        value = block_grads(factors[i], payload_refs, words_ref)
        outs[i][...] = olds[i][...] + value if adds else value


VMEM = pl.BlockSpec(memory_space=pltpu.VMEM)
SMEM = pl.BlockSpec(memory_space=pltpu.SMEM)
ANY = pl.BlockSpec(memory_space=pl.ANY)


def add_grads(where, blocks, factors, payloads, olds=()):
    rows = factors[0].shape[0]
    pairs = sum(payload.shape[0] for payload in payloads) // 2
    work = len(blocks) * rows * pairs * 2 * OWN
    count = len(blocks)
    return pl.pallas_call(
        functools.partial(grads_kernel, blocks, len(payloads), bool(olds)),
        out_shape=[jax.ShapeDtypeStruct((rows, 256), jnp.float32)] * count,
        in_specs=[SMEM] + [VMEM] * (count + len(payloads) + len(olds)),
        out_specs=[VMEM] * count,
        input_output_aliases=(
            {1 + count + len(payloads) + i: i for i in range(count)} if olds else {}
        ),
        scratch_shapes=[
            pltpu.VMEM((pairs, rows // 32, 128), jnp.int32),
            pltpu.VMEM((pairs, SLOTS, 128), jnp.int32),
            pltpu.VMEM((pairs, SLOTS, 128), jnp.int32),
        ],
        compiler_params=pltpu.CompilerParams(vmem_limit_bytes=32 * 1024 * 1024),
        cost_estimate=pl.CostEstimate(
            flops=4 * work * 256, bytes_accessed=1 << 22, transcendentals=work
        ),
    )(where, *factors, *payloads, *olds)


def join_kernel(*refs):
    pieces, out, sem = refs[:-2], refs[-2], refs[-1]
    spot, copies = 0, []
    for i, ref in enumerate(pieces):
        count = ref.shape[0]
        copies.append(pltpu.make_async_copy(ref, out.at[pl.ds(spot, count)], sem.at[i]))
        spot += count
    for copy in copies:
        copy.start()
    for copy in copies:
        copy.wait()


def join(*pieces):
    count = sum(piece.shape[0] for piece in pieces)
    return pl.pallas_call(
        join_kernel,
        out_shape=jax.ShapeDtypeStruct((count,) + pieces[0].shape[1:], pieces[0].dtype),
        in_specs=[ANY] * len(pieces),
        out_specs=VMEM,
        scratch_shapes=[pltpu.SemaphoreType.DMA((len(pieces),))],
    )(*pieces)


def combine_kernel(where_ref, mine_ref, other_ref, own_ref, *sends):
    quarter = own_ref.shape[0]

    def rows(step):
        start = pl.multiple_of(((where_ref[3] + step) & 3) * quarter, quarter)
        return mine_ref[pl.ds(start, quarter), :] + other_ref[pl.ds(start, quarter), :]

    for step, send in enumerate(sends):
        send[...] = rows(step + 1).astype(send.dtype)
    own_ref[...] = rows(0)


def combine(where, mine, other):
    shape = (mine.shape[0] // 4, mine.shape[1])
    return pl.pallas_call(
        combine_kernel,
        out_shape=[jax.ShapeDtypeStruct(shape, jnp.float32)]
        + [jax.ShapeDtypeStruct(shape, jnp.bfloat16)] * 3,
        in_specs=[SMEM, VMEM, VMEM],
        out_specs=[VMEM] * 4,
    )(where, mine, other)


def swap(value, axis, bit):
    size = lax.axis_size(axis)
    return lax.ppermute(value, axis, [(i, i ^ bit) for i in range(size)])


def shift_by(value, axis, step, inner=1):
    size = lax.axis_size(axis)
    return lax.ppermute(value, axis, [(i, (i + step * inner) % size) for i in range(size)])


def shards(queries, basis, factors, positives, counts, placement):
    label, dp, part = lax.axis_index("label"), lax.axis_index("dp"), lax.axis_index("basis")
    block = factors.shape[0] // lax.axis_size("dp")
    half = (dp & 1) * OWN
    mine = lax.dynamic_slice_in_dim(factors, dp * block, block, 0)
    partial_value = lax.dot_general(
        queries, basis, (((1,), (1,)), ((), ())), preferred_element_type=jnp.float32
    )
    others = swap(mine, "label", 1)
    digits = pl.pallas_call(
        digits_kernel,
        out_shape=jax.ShapeDtypeStruct((EXTRA, 256), jnp.bfloat16),
        in_specs=[SMEM, VMEM, VMEM, VMEM],
        out_specs=VMEM,
        cost_estimate=pl.CostEstimate(flops=1 << 31, bytes_accessed=1 << 19, transcendentals=0),
    )(
        jnp.stack([(half - part * OWN) & 255, half]).astype(jnp.int32),
        positives.T,
        counts.reshape(1, -1),
        placement.reshape(-1, 128),
    )

    rows = partial_value
    for bit in (2, 1):
        count = rows.shape[0] // 2
        high = (part >> (bit - 1)) & 1
        keep = lax.dynamic_slice_in_dim(rows, high * count, count, 0)
        send = lax.dynamic_slice_in_dim(rows, (1 - high) * count, count, 0)
        rows = keep + swap(send, "basis", bit)
    own = jnp.concatenate([rows.astype(jnp.bfloat16), digits], axis=0)[None]
    pair = join(own, swap(own, "dp", 1))
    ring = join(pair, *(shift_by(pair, "dp", step) for step in (2, 6, 4)))

    first = label * factors.shape[0] + dp * block
    other = (label ^ 1) * factors.shape[0] + dp * block
    where = jnp.stack([first, other, half, part]).astype(jnp.int32)
    above, below, across = (shift_by(ring, "label", step, 2) for step in (1, 3, 2))
    sum_mine, sum_other = add_grads(where, (0, 1), (mine, others), (ring,))
    (sum_other,) = add_grads(where, (1,), (others,), (above, below), (sum_other,))
    (sum_other,) = add_grads(where, (1,), (others,), (across,), (sum_other,))
    received = swap(sum_other, "label", 1)
    (sum_mine,) = add_grads(where, (0,), (mine,), (above, below, across), (sum_mine,))
    total, *sends = combine(where, sum_mine, received)
    for step in (2, 1, 3):
        total = total + shift_by(sends[step - 1], "basis", step).astype(jnp.float32)
    return total * SCALE


def solution(mesh):
    placed = (
        P(("label", "dp"), "basis"),
        P(None, "basis"),
        P("label", None),
        P(("label", "dp"), None),
        P(("label", "dp")),
        P(),
    )
    return jax.shard_map(
        shards,
        mesh=mesh,
        in_specs=placed,
        out_specs=P(("label", "dp", "basis"), None),
        check_vma=False,
    )
```

```python
import functools

import jax
import jax.numpy as jnp
from jax import lax
from jax.experimental import pallas as pl
from jax.experimental.pallas import tpu as pltpu
from jax.sharding import PartitionSpec as P


SLOTS = 16
OWN = 64
EXTRA = 16
PAIR = 2 * OWN
MIDDLE = 192
SCALE = 1.0 / 256.0
LINK = jnp.bfloat16
NOWHERE = -250.0


def digits_kernel(where_ref, pos_ref, counts_ref, place_ref, out_ref):
    shift, half = where_ref[0], where_ref[1]
    table = place_ref[...]
    high = ((table >> 8) - MIDDLE).astype(jnp.float32).astype(jnp.bfloat16)
    low = (table & 255).astype(jnp.float32).astype(jnp.bfloat16)
    tables = jnp.concatenate([high, low], axis=1)
    pos = pltpu.roll(pos_ref[...], shift, 1)[:, :128]
    counts = pltpu.roll(jnp.broadcast_to(counts_ref[...], (8, 256)), shift, 1)[0:1, :128]
    groups = table.shape[0]
    row = lax.broadcasted_iota(jnp.int32, (groups, 128), 0)
    lane = lax.broadcasted_iota(jnp.int32, (128, 128), 0)
    spot = lax.broadcasted_iota(jnp.int32, (1, 128), 1)
    mine = (spot >= half) & (spot < half + OWN)
    highs, lows = [], []
    for k in range(SLOTS):
        one = pos[k : k + 1, :]
        hot = jnp.where(row == (one >> 7), 1.0, 0.0).astype(jnp.bfloat16)
        both = lax.dot_general(tables, hot, (((0,), (0,)), ((), ())), preferred_element_type=jnp.float32)
        pick = lane == (one & 127)
        first = jnp.sum(jnp.where(pick, both[:128], 0.0), axis=0, keepdims=True)
        second = jnp.sum(jnp.where(pick, both[128:], 0.0), axis=0, keepdims=True)
        used = k < counts
        highs.append(jnp.where(mine, jnp.where(used, first, NOWHERE), 0.0))
        lows.append(jnp.where(mine & used, second, 0.0))
    out_ref[...] = jnp.concatenate(
        [jnp.concatenate(highs, axis=0), jnp.concatenate(lows, axis=0)], axis=1
    ).astype(jnp.bfloat16)


def build_words(base, payload_refs, words_ref, word_ref, bit_ref):
    spot = 0
    for payload_ref in payload_refs:
        for p in range(payload_ref.shape[0]):
            both = payload_ref[p, PAIR:, :].astype(jnp.float32).astype(jnp.int32)
            local = (both[:, :128] + MIDDLE) * 256 + both[:, 128:] - base
            word_ref[spot] = local >> 5
            bit_ref[spot] = jnp.left_shift(1, local & 31)
            spot += 1
    shape = words_ref.shape[1:]
    order = lax.broadcasted_iota(jnp.int32, shape, 0)

    def build(p, carry):
        found = jnp.zeros(shape, jnp.int32)
        for k in range(SLOTS):
            word = jnp.broadcast_to(word_ref[p, k : k + 1, :], shape)
            bit = jnp.broadcast_to(bit_ref[p, k : k + 1, :], shape)
            found = found | jnp.where(order == word, bit, 0)
        words_ref[p] = found
        return carry

    lax.fori_loop(0, spot, build, 0)


def block_grads(factor_ref, payload_refs, words_ref):
    word_count = words_ref.shape[1]
    bits = jnp.left_shift(1, lax.broadcasted_iota(jnp.int32, (32, 128), 0))
    proj = [ref[:, :PAIR, :].reshape(-1, 256) for ref in payload_refs]
    proj = proj[0] if len(proj) == 1 else jnp.concatenate(proj, axis=0)
    scores = lax.dot_general(
        factor_ref[...],
        proj * jnp.bfloat16(0.5),
        (((1,), (1,)), ((), ())),
        preferred_element_type=jnp.float32,
    )
    tanh = jnp.tanh(scores)
    columns = []
    for c in range(proj.shape[0] // 128):
        found = words_ref[c]
        rows = []
        for m in range(word_count):
            hit = (jnp.broadcast_to(found[m : m + 1, :], (32, 128)) & bits) != 0
            piece = tanh[m * 32 : m * 32 + 32, c * 128 : c * 128 + 128]
            rows.append((piece + jnp.where(hit, -1.0, 1.0)).astype(jnp.bfloat16))
        columns.append(jnp.concatenate(rows, axis=0))
    grad = jnp.concatenate(columns, axis=1)
    return jnp.dot(grad, proj, preferred_element_type=jnp.float32)


def grads_kernel(blocks, payloads, adds, where_ref, *refs):
    count = len(blocks)
    given = count + payloads + count * adds
    sources, refs = refs[:given], refs[given:]
    outs, refs = refs[:count], refs[count:]
    held, (words_ref, word_ref, bit_ref, sem) = refs[:given], refs[given:]
    copies = [
        pltpu.make_async_copy(source, hold, sem.at[i])
        for i, (source, hold) in enumerate(zip(sources, held))
    ]
    payload_refs = held[count : count + payloads]
    for copy in copies[count : count + payloads] + copies[:count] + copies[count + payloads :]:
        copy.start()
    for copy in copies[count : count + payloads]:
        copy.wait()
    for i, which in enumerate(blocks):
        build_words(where_ref[which], payload_refs, words_ref, word_ref, bit_ref)
        copies[i].wait()
        value = block_grads(held[i], payload_refs, words_ref)
        if adds:
            copies[count + payloads + i].wait()
            value = held[count + payloads + i][...] + value
        outs[i][...] = value


VMEM = pl.BlockSpec(memory_space=pltpu.VMEM)
SMEM = pl.BlockSpec(memory_space=pltpu.SMEM)
ANY = pl.BlockSpec(memory_space=pl.ANY)


def add_grads(where, blocks, factors, payloads, olds=()):
    rows = factors[0].shape[0]
    pairs = sum(payload.shape[0] for payload in payloads)
    work = len(blocks) * rows * pairs * PAIR
    operands = (*factors, *payloads, *olds)
    return pl.pallas_call(
        functools.partial(grads_kernel, blocks, len(payloads), bool(olds)),
        out_shape=[jax.ShapeDtypeStruct((rows, 256), jnp.float32)] * len(blocks),
        in_specs=[SMEM] + [ANY] * len(operands),
        out_specs=[VMEM] * len(blocks),
        scratch_shapes=[pltpu.VMEM(operand.shape, operand.dtype) for operand in operands]
        + [
            pltpu.VMEM((pairs, rows // 32, 128), jnp.int32),
            pltpu.VMEM((pairs, SLOTS, 128), jnp.int32),
            pltpu.VMEM((pairs, SLOTS, 128), jnp.int32),
            pltpu.SemaphoreType.DMA((len(operands),)),
        ],
        compiler_params=pltpu.CompilerParams(vmem_limit_bytes=60 * 1024 * 1024),
        cost_estimate=pl.CostEstimate(
            flops=4 * work * 256, bytes_accessed=1 << 22, transcendentals=work
        ),
    )(where, *operands)


def swap(value, axis, bit):
    size = lax.axis_size(axis)
    return lax.ppermute(value, axis, [(i, i ^ bit) for i in range(size)])


def shift_by(value, axis, step, inner=1):
    size = lax.axis_size(axis)
    return lax.ppermute(value, axis, [(i, (i + step * inner) % size) for i in range(size)])


def body(queries, basis, factors, positives, counts, placement):
    label, dp, part = lax.axis_index("label"), lax.axis_index("dp"), lax.axis_index("basis")
    block = factors.shape[0] // lax.axis_size("dp")
    half = (dp & 1) * OWN
    mine = lax.dynamic_slice_in_dim(factors, dp * block, block, 0)
    partial_value = lax.dot_general(
        queries, basis, (((1,), (1,)), ((), ())), preferred_element_type=jnp.float32
    )
    others = swap(mine, "label", 1)
    digits = pl.pallas_call(
        digits_kernel,
        out_shape=jax.ShapeDtypeStruct((EXTRA, 256), jnp.bfloat16),
        in_specs=[SMEM, VMEM, VMEM, VMEM],
        out_specs=VMEM,
        cost_estimate=pl.CostEstimate(flops=1 << 31, bytes_accessed=1 << 19, transcendentals=0),
    )(
        jnp.stack([(half - part * OWN) & 255, half]).astype(jnp.int32),
        positives.T,
        counts.reshape(1, -1),
        placement.reshape(-1, 128),
    )

    rows = partial_value
    for bit in (2, 1):
        count = rows.shape[0] // 2
        high = (part >> (bit - 1)) & 1
        keep = lax.dynamic_slice_in_dim(rows, high * count, count, 0)
        send = lax.dynamic_slice_in_dim(rows, (1 - high) * count, count, 0)
        rows = keep + swap(send, "basis", bit)
    own = jnp.concatenate([rows.astype(jnp.bfloat16), digits], axis=0)
    next_own = swap(own, "dp", 1)
    even = dp & 1 == 0
    pair = jnp.concatenate(
        [
            jnp.where(even, own[:OWN], next_own[:OWN]),
            jnp.where(even, next_own[:OWN], own[:OWN]),
            own[OWN:] + next_own[OWN:],
        ],
        axis=0,
    )[None]
    ring = jnp.concatenate([pair] + [shift_by(pair, "dp", step) for step in (2, 6, 4)], axis=0)

    first = label * factors.shape[0] + dp * block
    other = (label ^ 1) * factors.shape[0] + dp * block
    where = jnp.stack([first, other]).astype(jnp.int32)
    half_ring = ring.shape[0] // 2
    near = [shift_by(ring, "label", step, 2) for step in (1, 3)]
    far = [
        shift_by(near[0][:half_ring], "label", 1, 2),
        shift_by(near[1][half_ring:], "label", 3, 2),
    ]
    sum_mine, sum_other = add_grads(where, (0, 1), (mine, others), (ring,))
    (sum_other,) = add_grads(where, (1,), (others,), near, (sum_other,))
    (sum_other,) = add_grads(where, (1,), (others,), far, (sum_other,))
    received = swap(sum_other, "label", 1)
    (sum_mine,) = add_grads(where, (0,), (mine,), near + far, (sum_mine,))

    quarter = block // lax.axis_size("basis")

    def quarter_of(step):
        start = ((part + step) & 3) * quarter
        return lax.dynamic_slice_in_dim(sum_mine, start, quarter, 0) + lax.dynamic_slice_in_dim(
            received, start, quarter, 0
        )

    total = quarter_of(0)
    for step in (2, 1, 3):
        sent = (quarter_of(step) * SCALE).astype(LINK)
        total = total + shift_by(sent, "basis", step).astype(jnp.float32) * (1 / SCALE)
    return total * SCALE


def solution(mesh):
    placed = (
        P(("label", "dp"), "basis"),
        P(None, "basis"),
        P("label", None),
        P(("label", "dp"), None),
        P(("label", "dp")),
        P(),
    )
    return jax.shard_map(
        body,
        mesh=mesh,
        in_specs=placed,
        out_specs=P(("label", "dp", "basis"), None),
        check_vma=False,
    )
```

```python
import functools

import jax
import jax.numpy as jnp
from jax import lax
from jax.experimental import pallas as pl
from jax.experimental.pallas import tpu as pltpu
from jax.sharding import PartitionSpec as P


SLOTS = 16
OWN = 64
EXTRA = 16
PAIR = 2 * OWN
MIDDLE = 192
SCALE = 1.0 / 256.0
GRANT = 8
LINK = jnp.float16
NOWHERE = -250.0


def digits_kernel(where_ref, pos_ref, counts_ref, place_ref, out_ref):
    shift, half = where_ref[0], where_ref[1]
    table = place_ref[...]
    high = ((table >> 8) - MIDDLE).astype(jnp.float32).astype(jnp.bfloat16)
    low = (table & 255).astype(jnp.float32).astype(jnp.bfloat16)
    tables = jnp.concatenate([high, low], axis=1)
    pos = pltpu.roll(pos_ref[...], shift, 1)[:, :128]
    counts = pltpu.roll(jnp.broadcast_to(counts_ref[...], (8, 256)), shift, 1)[0:1, :128]
    groups = table.shape[0]
    row = lax.broadcasted_iota(jnp.int32, (groups, 128), 0)
    lane = lax.broadcasted_iota(jnp.int32, (128, 128), 0)
    spot = lax.broadcasted_iota(jnp.int32, (1, 128), 1)
    mine = (spot >= half) & (spot < half + OWN)
    highs, lows = [], []
    for k in range(SLOTS):
        one = pos[k : k + 1, :]
        hot = jnp.where(row == (one >> 7), 1.0, 0.0).astype(jnp.bfloat16)
        both = lax.dot_general(tables, hot, (((0,), (0,)), ((), ())), preferred_element_type=jnp.float32)
        pick = lane == (one & 127)
        first = jnp.sum(jnp.where(pick, both[:128], 0.0), axis=0, keepdims=True)
        second = jnp.sum(jnp.where(pick, both[128:], 0.0), axis=0, keepdims=True)
        used = k < counts
        highs.append(jnp.where(mine, jnp.where(used, first, NOWHERE), 0.0))
        lows.append(jnp.where(mine & used, second, 0.0))
    out_ref[...] = jnp.concatenate(
        [jnp.concatenate(highs, axis=0), jnp.concatenate(lows, axis=0)], axis=1
    ).astype(jnp.bfloat16)


def build_words(base, payload_refs, words_ref, word_ref, bit_ref):
    spot = 0
    for payload_ref in payload_refs:
        for p in range(payload_ref.shape[0]):
            both = payload_ref[p, PAIR:, :].astype(jnp.float32).astype(jnp.int32)
            local = (both[:, :128] + MIDDLE) * 256 + both[:, 128:] - base
            word_ref[spot] = local >> 5
            bit_ref[spot] = jnp.left_shift(1, local & 31)
            spot += 1
    shape = words_ref.shape[1:]
    order = lax.broadcasted_iota(jnp.int32, shape, 0)

    def build(p, carry):
        found = jnp.zeros(shape, jnp.int32)
        for k in range(SLOTS):
            word = jnp.broadcast_to(word_ref[p, k : k + 1, :], shape)
            bit = jnp.broadcast_to(bit_ref[p, k : k + 1, :], shape)
            found = found | jnp.where(order == word, bit, 0)
        words_ref[p] = found
        return carry

    lax.fori_loop(0, spot, build, 0)


def block_grads(factor_ref, payload_refs, words_ref):
    word_count = words_ref.shape[1]
    bits = jnp.left_shift(1, lax.broadcasted_iota(jnp.int32, (32, 128), 0))
    proj = [ref[:, :PAIR, :].reshape(-1, 256) for ref in payload_refs]
    proj = proj[0] if len(proj) == 1 else jnp.concatenate(proj, axis=0)
    scores = lax.dot_general(
        factor_ref[...],
        proj * jnp.bfloat16(0.5),
        (((1,), (1,)), ((), ())),
        preferred_element_type=jnp.float32,
    )
    tanh = jnp.tanh(scores)
    columns = []
    for c in range(proj.shape[0] // 128):
        found = words_ref[c]
        rows = []
        for m in range(word_count):
            hit = (jnp.broadcast_to(found[m : m + 1, :], (32, 128)) & bits) != 0
            piece = tanh[m * 32 : m * 32 + 32, c * 128 : c * 128 + 128]
            rows.append((piece + jnp.where(hit, -1.0, 1.0)).astype(jnp.bfloat16))
        columns.append(jnp.concatenate(rows, axis=0))
    grad = jnp.concatenate(columns, axis=1)
    return jnp.dot(grad, proj, preferred_element_type=jnp.float32)


def grads_kernel(blocks, payloads, adds, where_ref, *refs):
    count = len(blocks)
    factors, refs = refs[:count], refs[count:]
    payload_refs, refs = refs[:payloads], refs[payloads:]
    olds, refs = refs[: count * adds], refs[count * adds :]
    outs, (words_ref, word_ref, bit_ref) = refs[:count], refs[count:]
    for i, which in enumerate(blocks):
        build_words(where_ref[which], payload_refs, words_ref, word_ref, bit_ref)
        value = block_grads(factors[i], payload_refs, words_ref)
        outs[i][...] = olds[i][...] + value if adds else value


VMEM = pl.BlockSpec(memory_space=pltpu.VMEM)
SMEM = pl.BlockSpec(memory_space=pltpu.SMEM)


def add_grads(where, blocks, factors, payloads, olds=()):
    rows = factors[0].shape[0]
    pairs = sum(payload.shape[0] for payload in payloads)
    work = len(blocks) * rows * pairs * PAIR
    return pl.pallas_call(
        functools.partial(grads_kernel, blocks, len(payloads), bool(olds)),
        out_shape=[jax.ShapeDtypeStruct((rows, 256), jnp.float32)] * len(blocks),
        in_specs=[SMEM] + [VMEM] * (len(blocks) + len(payloads) + len(olds)),
        out_specs=[VMEM] * len(blocks),
        scratch_shapes=[
            pltpu.VMEM((pairs, rows // 32, 128), jnp.int32),
            pltpu.VMEM((pairs, SLOTS, 128), jnp.int32),
            pltpu.VMEM((pairs, SLOTS, 128), jnp.int32),
        ],
        compiler_params=pltpu.CompilerParams(vmem_limit_bytes=GRANT * 1024 * 1024),
        cost_estimate=pl.CostEstimate(
            flops=4 * work * 256, bytes_accessed=1 << 22, transcendentals=work
        ),
    )(where, *factors, *payloads, *olds)


def swap(value, axis, bit):
    size = lax.axis_size(axis)
    return lax.ppermute(value, axis, [(i, i ^ bit) for i in range(size)])


def shift_by(value, axis, step, inner=1):
    size = lax.axis_size(axis)
    return lax.ppermute(value, axis, [(i, (i + step * inner) % size) for i in range(size)])


def turn(value, step):
    size = lax.axis_size("label")
    return lax.ppermute(
        value, "label", [(i, (i + (2 - 4 * (i % 2)) * step) % size) for i in range(size)]
    )


def body(queries, basis, factors, positives, counts, placement):
    label, dp, part = lax.axis_index("label"), lax.axis_index("dp"), lax.axis_index("basis")
    block = factors.shape[0] // lax.axis_size("dp")
    half = (dp & 1) * OWN
    mine = lax.dynamic_slice_in_dim(factors, dp * block, block, 0)
    partial_value = lax.dot_general(
        queries, basis, (((1,), (1,)), ((), ())), preferred_element_type=jnp.float32
    )
    others = swap(mine, "label", 1)
    digits = pl.pallas_call(
        digits_kernel,
        out_shape=jax.ShapeDtypeStruct((EXTRA, 256), jnp.bfloat16),
        in_specs=[SMEM, VMEM, VMEM, VMEM],
        out_specs=VMEM,
        cost_estimate=pl.CostEstimate(
            flops=1 << 31, bytes_accessed=1 << 19, transcendentals=0
        ),
    )(
        jnp.stack([(half - part * OWN) & 255, half]).astype(jnp.int32),
        positives.T,
        counts.reshape(1, -1),
        placement.reshape(-1, 128),
    )

    def piece_of(value, step):
        count = value.shape[0] // lax.axis_size("basis")
        return lax.dynamic_slice_in_dim(value, ((part + step) & 3) * count, count, 0)

    rows = piece_of(partial_value, 0)
    moved = [shift_by(piece_of(partial_value, step), "basis", step) for step in (2, 1, 3)]
    for value in moved:
        rows = rows + value
    own = jnp.concatenate([rows.astype(jnp.bfloat16), digits], axis=0)
    next_own = swap(own, "dp", 1)
    even = dp & 1 == 0
    pair = jnp.concatenate(
        [
            jnp.where(even, own[:OWN], next_own[:OWN]),
            jnp.where(even, next_own[:OWN], own[:OWN]),
            own[OWN:] + next_own[OWN:],
        ],
        axis=0,
    )[None]
    ring = jnp.concatenate([pair] + [shift_by(pair, "dp", step) for step in (2, 6, 4)], axis=0)

    first = label * factors.shape[0] + dp * block
    other = (label ^ 1) * factors.shape[0] + dp * block
    where = jnp.stack([first, other]).astype(jnp.int32)
    near = [turn(ring, 1), turn(ring, -1)]
    far = [turn(near[0], 1)]
    sum_mine, sum_other = add_grads(where, (0, 1), (mine, others), (ring,))
    (sum_other,) = add_grads(where, (1,), (others,), near, (sum_other,))
    (sum_other,) = add_grads(where, (1,), (others,), far, (sum_other,))
    received = swap(sum_other, "label", 1)
    (sum_mine,) = add_grads(where, (0,), (mine,), near + far, (sum_mine,))

    order = (2, 1, 3)
    quarters = [piece_of(sum_mine, step) + piece_of(received, step) for step in (0,) + order]
    total, *sent = lax.optimization_barrier(
        (quarters[0], *((value * SCALE).astype(LINK) for value in quarters[1:]))
    )
    total = total * SCALE
    for i, step in enumerate(order):
        total = total + shift_by(sent[i], "basis", step).astype(jnp.float32)
        if i == 0:
            total = lax.optimization_barrier(total)
    return total


def solution(mesh):
    placed = (
        P(("label", "dp"), "basis"),
        P(None, "basis"),
        P("label", None),
        P(("label", "dp"), None),
        P(("label", "dp")),
        P(),
    )
    return jax.shard_map(
        body,
        mesh=mesh,
        in_specs=placed,
        out_specs=P(("label", "dp", "basis"), None),
        check_vma=False,
    )
```

```python
import functools

import jax
import jax.numpy as jnp
from jax import lax
from jax.experimental import pallas as pl
from jax.experimental.pallas import tpu as pltpu
from jax.sharding import PartitionSpec as P


SLOTS = 16
OWN = 64
EXTRA = 16
PAIR = 2 * OWN
MIDDLE = 192
SCALE = 1.0 / 256.0
GRANT = 8
LINK = jnp.float16
NOWHERE = -250.0


def digits_kernel(where_ref, pos_ref, counts_ref, place_ref, out_ref):
    shift, half = where_ref[0], where_ref[1]
    table = place_ref[...]
    high = ((table >> 8) - MIDDLE).astype(jnp.float32).astype(jnp.bfloat16)
    low = (table & 255).astype(jnp.float32).astype(jnp.bfloat16)
    tables = jnp.concatenate([high, low], axis=1)
    pos = pltpu.roll(pos_ref[...], shift, 1)[:, :128]
    counts = pltpu.roll(jnp.broadcast_to(counts_ref[...], (8, 256)), shift, 1)[0:1, :128]
    groups = table.shape[0]
    row = lax.broadcasted_iota(jnp.int32, (groups, 128), 0)
    lane = lax.broadcasted_iota(jnp.int32, (128, 128), 0)
    spot = lax.broadcasted_iota(jnp.int32, (1, 128), 1)
    mine = (spot >= half) & (spot < half + OWN)
    highs, lows = [], []
    for k in range(SLOTS):
        one = pos[k : k + 1, :]
        hot = jnp.where(row == (one >> 7), 1.0, 0.0).astype(jnp.bfloat16)
        both = lax.dot_general(tables, hot, (((0,), (0,)), ((), ())), preferred_element_type=jnp.float32)
        pick = lane == (one & 127)
        first = jnp.sum(jnp.where(pick, both[:128], 0.0), axis=0, keepdims=True)
        second = jnp.sum(jnp.where(pick, both[128:], 0.0), axis=0, keepdims=True)
        used = k < counts
        highs.append(jnp.where(mine, jnp.where(used, first, NOWHERE), 0.0))
        lows.append(jnp.where(mine & used, second, 0.0))
    out_ref[...] = jnp.concatenate(
        [jnp.concatenate(highs, axis=0), jnp.concatenate(lows, axis=0)], axis=1
    ).astype(jnp.bfloat16)


def build_words(base, payload_refs, words_ref, word_ref, bit_ref):
    spot = 0
    for payload_ref in payload_refs:
        for p in range(payload_ref.shape[0]):
            both = payload_ref[p, PAIR:, :].astype(jnp.float32).astype(jnp.int32)
            local = (both[:, :128] + MIDDLE) * 256 + both[:, 128:] - base
            word_ref[spot] = local >> 5
            bit_ref[spot] = jnp.left_shift(1, local & 31)
            spot += 1
    shape = words_ref.shape[1:]
    order = lax.broadcasted_iota(jnp.int32, shape, 0)

    def build(p, carry):
        found = jnp.zeros(shape, jnp.int32)
        for k in range(SLOTS):
            word = jnp.broadcast_to(word_ref[p, k : k + 1, :], shape)
            bit = jnp.broadcast_to(bit_ref[p, k : k + 1, :], shape)
            found = found | jnp.where(order == word, bit, 0)
        words_ref[p] = found
        return carry

    lax.fori_loop(0, spot, build, 0)


def block_grads(factor_ref, payload_refs, words_ref):
    word_count = words_ref.shape[1]
    bits = jnp.left_shift(1, lax.broadcasted_iota(jnp.int32, (32, 128), 0))
    proj = [ref[:, :PAIR, :].reshape(-1, 256) for ref in payload_refs]
    proj = proj[0] if len(proj) == 1 else jnp.concatenate(proj, axis=0)
    scores = lax.dot_general(
        factor_ref[...],
        proj * jnp.bfloat16(0.5),
        (((1,), (1,)), ((), ())),
        preferred_element_type=jnp.float32,
    )
    tanh = jnp.tanh(scores)
    columns = []
    for c in range(proj.shape[0] // 128):
        found = words_ref[c]
        rows = []
        for m in range(word_count):
            hit = (jnp.broadcast_to(found[m : m + 1, :], (32, 128)) & bits) != 0
            piece = tanh[m * 32 : m * 32 + 32, c * 128 : c * 128 + 128]
            rows.append((piece + jnp.where(hit, -1.0, 1.0)).astype(jnp.bfloat16))
        columns.append(jnp.concatenate(rows, axis=0))
    grad = jnp.concatenate(columns, axis=1)
    return jnp.dot(grad, proj, preferred_element_type=jnp.float32)


def grads_kernel(blocks, payloads, adds, where_ref, *refs):
    count = len(blocks)
    factors, refs = refs[:count], refs[count:]
    payload_refs, refs = refs[:payloads], refs[payloads:]
    olds, refs = refs[: count * adds], refs[count * adds :]
    outs, (words_ref, word_ref, bit_ref) = refs[:count], refs[count:]
    for i, which in enumerate(blocks):
        build_words(where_ref[which], payload_refs, words_ref, word_ref, bit_ref)
        value = block_grads(factors[i], payload_refs, words_ref)
        outs[i][...] = olds[i][...] + value if adds else value


VMEM = pl.BlockSpec(memory_space=pltpu.VMEM)
SMEM = pl.BlockSpec(memory_space=pltpu.SMEM)


def add_grads(where, blocks, factors, payloads, olds=()):
    rows = factors[0].shape[0]
    pairs = sum(payload.shape[0] for payload in payloads)
    work = len(blocks) * rows * pairs * PAIR
    return pl.pallas_call(
        functools.partial(grads_kernel, blocks, len(payloads), bool(olds)),
        out_shape=[jax.ShapeDtypeStruct((rows, 256), jnp.float32)] * len(blocks),
        in_specs=[SMEM] + [VMEM] * (len(blocks) + len(payloads) + len(olds)),
        out_specs=[VMEM] * len(blocks),
        scratch_shapes=[
            pltpu.VMEM((pairs, rows // 32, 128), jnp.int32),
            pltpu.VMEM((pairs, SLOTS, 128), jnp.int32),
            pltpu.VMEM((pairs, SLOTS, 128), jnp.int32),
        ],
        compiler_params=pltpu.CompilerParams(vmem_limit_bytes=GRANT * 1024 * 1024),
        cost_estimate=pl.CostEstimate(
            flops=4 * work * 256, bytes_accessed=1 << 22, transcendentals=work
        ),
    )(where, *factors, *payloads, *olds)


def swap(value, axis, bit):
    size = lax.axis_size(axis)
    return lax.ppermute(value, axis, [(i, i ^ bit) for i in range(size)])


def shift_by(value, axis, step, inner=1):
    size = lax.axis_size(axis)
    return lax.ppermute(value, axis, [(i, (i + step * inner) % size) for i in range(size)])


def turn(value, step):
    size = lax.axis_size("label")
    return lax.ppermute(
        value, "label", [(i, (i + (2 - 4 * (i % 2)) * step) % size) for i in range(size)]
    )


def body(queries, basis, factors, positives, counts, placement):
    label, dp, part = lax.axis_index("label"), lax.axis_index("dp"), lax.axis_index("basis")
    block = factors.shape[0] // lax.axis_size("dp")
    half = (dp & 1) * OWN
    mine = lax.dynamic_slice_in_dim(factors, dp * block, block, 0)
    partial_value = lax.dot_general(
        queries, basis, (((1,), (1,)), ((), ())), preferred_element_type=jnp.float32
    )
    others = swap(mine, "label", 1)
    digits = pl.pallas_call(
        digits_kernel,
        out_shape=jax.ShapeDtypeStruct((EXTRA, 256), jnp.bfloat16),
        in_specs=[SMEM, VMEM, VMEM, VMEM],
        out_specs=VMEM,
        cost_estimate=pl.CostEstimate(
            flops=1 << 31, bytes_accessed=1 << 19, transcendentals=0
        ),
    )(
        jnp.stack([(half - part * OWN) & 255, half]).astype(jnp.int32),
        positives.T,
        counts.reshape(1, -1),
        placement.reshape(-1, 128),
    )

    def piece_of(value, step):
        count = value.shape[0] // lax.axis_size("basis")
        return lax.dynamic_slice_in_dim(value, ((part + step) & 3) * count, count, 0)

    rows = piece_of(partial_value, 0)
    moved = [shift_by(piece_of(partial_value, step), "basis", step) for step in (2, 1, 3)]
    for value in moved:
        rows = rows + value
    own = jnp.concatenate([rows.astype(jnp.bfloat16), digits], axis=0)
    next_own = swap(own, "dp", 1)
    even = dp & 1 == 0
    pair = jnp.concatenate(
        [
            jnp.where(even, own[:OWN], next_own[:OWN]),
            jnp.where(even, next_own[:OWN], own[:OWN]),
            own[OWN:] + next_own[OWN:],
        ],
        axis=0,
    )[None]
    ring = jnp.concatenate([pair] + [shift_by(pair, "dp", step) for step in (2, 6, 4)], axis=0)

    first = label * factors.shape[0] + dp * block
    other = (label ^ 1) * factors.shape[0] + dp * block
    where = jnp.stack([first, other]).astype(jnp.int32)
    near = [turn(ring, 1), turn(ring, -1)]
    far = [turn(near[0], 1)]
    sum_mine, sum_other = add_grads(where, (0, 1), (mine, others), (ring,))
    sum_other, sum_mine = add_grads(
        where, (1, 0), (others, mine), near, (sum_other, sum_mine)
    )
    (sum_other,) = add_grads(where, (1,), (others,), far, (sum_other,))
    received = swap(sum_other, "label", 1)
    (sum_mine,) = add_grads(where, (0,), (mine,), far, (sum_mine,))

    order = (2, 1, 3)
    quarters = [piece_of(sum_mine, step) + piece_of(received, step) for step in (0,) + order]
    total, *sent = lax.optimization_barrier(
        (quarters[0], *((value * SCALE).astype(LINK) for value in quarters[1:]))
    )
    total = total * SCALE
    for i, step in enumerate(order):
        total = total + shift_by(sent[i], "basis", step).astype(jnp.float32)
        if i == 0:
            total = lax.optimization_barrier(total)
    return total


def solution(mesh):
    placed = (
        P(("label", "dp"), "basis"),
        P(None, "basis"),
        P("label", None),
        P(("label", "dp"), None),
        P(("label", "dp")),
        P(),
    )
    return jax.shard_map(
        body,
        mesh=mesh,
        in_specs=placed,
        out_specs=P(("label", "dp", "basis"), None),
        check_vma=False,
    )
```

```python
import functools

import jax
import jax.numpy as jnp
from jax import lax
from jax.experimental import pallas as pl
from jax.experimental.pallas import tpu as pltpu
from jax.sharding import PartitionSpec as P


SLOTS = 16
OWN = 64
EXTRA = 16
PAIR = 2 * OWN
MIDDLE = 192
SCALE = 1.0 / 256.0
GRANT = 8
LINK = jnp.float16
NOWHERE = -250.0


def digits_kernel(where_ref, pos_ref, counts_ref, place_ref, out_ref):
    start, half = where_ref[1], where_ref[2]
    table = place_ref[...]
    high = ((table >> 8) - MIDDLE).astype(jnp.float32).astype(jnp.bfloat16)
    low = (table & 255).astype(jnp.float32).astype(jnp.bfloat16)
    tables = jnp.concatenate([high, low], axis=1)
    count = SLOTS // 2
    lane = lax.broadcasted_iota(jnp.int32, (count, 128), 1)
    lower = lane < OWN
    early = pltpu.roll(pos_ref[:count, :], (256 - start) & 255, 1)[:, :128]
    late = pltpu.roll(pos_ref[count:, :], (256 + OWN - start) & 255, 1)[:, :128]
    pos = jnp.where(lower, early, late)
    groups = table.shape[0]
    row = lax.broadcasted_iota(jnp.int32, (groups, 256), 0)
    spot = lax.broadcasted_iota(jnp.int32, (128, 256), 0)
    firsts, seconds = [], []
    for k in range(count // 2):
        one = jnp.concatenate([pos[2 * k : 2 * k + 1, :], pos[2 * k + 1 : 2 * k + 2, :]], axis=1)
        hot = jnp.where(row == (one >> 7), 1.0, 0.0).astype(jnp.bfloat16)
        both = lax.dot_general(tables, hot, (((0,), (0,)), ((), ())), preferred_element_type=jnp.float32)
        pick = spot == (one & 127)
        first = jnp.sum(jnp.where(pick, both[:128], 0.0), axis=0, keepdims=True)
        second = jnp.sum(jnp.where(pick, both[128:], 0.0), axis=0, keepdims=True)
        firsts += [first[:, :128], first[:, 128:]]
        seconds += [second[:, :128], second[:, 128:]]
    first = jnp.concatenate(firsts, axis=0)
    second = jnp.concatenate(seconds, axis=0)
    counts = jnp.broadcast_to(counts_ref[...], (count, 256))
    counts = pltpu.roll(counts, (256 + half - start) & 255, 1)[:, :128]
    mine = (lane >= half) & (lane < half + OWN)
    slot = lax.broadcasted_iota(jnp.int32, (count, 128), 0)

    def placed(value, shift, used, nothing):
        return jnp.where(mine, jnp.where(used, pltpu.roll(value, shift, 1), nothing), 0.0)

    highs, lows = [], []
    for shift, base in ((half, 0), (OWN - half, count)):
        used = slot + base < counts
        highs.append(placed(first, shift, used, NOWHERE))
        lows.append(placed(second, shift, used, 0.0))
    out_ref[...] = jnp.concatenate(
        [jnp.concatenate(highs, axis=0), jnp.concatenate(lows, axis=0)], axis=1
    ).astype(jnp.bfloat16)


def build_words(base, payload_refs, words_ref, word_ref, bit_ref):
    spot = 0
    for payload_ref in payload_refs:
        for p in range(payload_ref.shape[0]):
            both = payload_ref[p, PAIR:, :].astype(jnp.float32).astype(jnp.int32)
            local = (both[:, :128] + MIDDLE) * 256 + both[:, 128:] - base
            word_ref[spot] = local >> 5
            bit_ref[spot] = jnp.left_shift(1, local & 31)
            spot += 1
    shape = words_ref.shape[1:]
    order = lax.broadcasted_iota(jnp.int32, shape, 0)

    def build(p, carry):
        found = jnp.zeros(shape, jnp.int32)
        for k in range(SLOTS):
            word = jnp.broadcast_to(word_ref[p, k : k + 1, :], shape)
            bit = jnp.broadcast_to(bit_ref[p, k : k + 1, :], shape)
            found = found | jnp.where(order == word, bit, 0)
        words_ref[p] = found
        return carry

    lax.fori_loop(0, spot, build, 0)


def block_grads(factor_ref, payload_refs, words_ref):
    word_count = words_ref.shape[1]
    bits = jnp.left_shift(1, lax.broadcasted_iota(jnp.int32, (32, 128), 0))
    proj = [ref[:, :PAIR, :].reshape(-1, 256) for ref in payload_refs]
    proj = proj[0] if len(proj) == 1 else jnp.concatenate(proj, axis=0)
    scores = lax.dot_general(
        factor_ref[...],
        proj * jnp.bfloat16(0.5),
        (((1,), (1,)), ((), ())),
        preferred_element_type=jnp.float32,
    )
    tanh = jnp.tanh(scores)
    columns = []
    for c in range(proj.shape[0] // 128):
        found = words_ref[c]
        rows = []
        for m in range(word_count):
            hit = (jnp.broadcast_to(found[m : m + 1, :], (32, 128)) & bits) != 0
            piece = tanh[m * 32 : m * 32 + 32, c * 128 : c * 128 + 128]
            rows.append((piece + jnp.where(hit, -1.0, 1.0)).astype(jnp.bfloat16))
        columns.append(jnp.concatenate(rows, axis=0))
    grad = jnp.concatenate(columns, axis=1)
    return jnp.dot(grad, proj, preferred_element_type=jnp.float32)


def grads_kernel(payloads, adds, where_ref, factor_ref, *refs):
    payload_refs, refs = refs[:payloads], refs[payloads:]
    olds, (out_ref, words_ref, word_ref, bit_ref) = refs[:adds], refs[adds:]
    build_words(where_ref[0], payload_refs, words_ref, word_ref, bit_ref)
    value = block_grads(factor_ref, payload_refs, words_ref)
    out_ref[...] = olds[0][...] + value if adds else value


VMEM = pl.BlockSpec(memory_space=pltpu.VMEM)
SMEM = pl.BlockSpec(memory_space=pltpu.SMEM)


def add_grads(where, factors, payloads, *olds):
    rows = factors.shape[0]
    pairs = sum(payload.shape[0] for payload in payloads)
    work = rows * pairs * PAIR
    return pl.pallas_call(
        functools.partial(grads_kernel, len(payloads), len(olds)),
        out_shape=jax.ShapeDtypeStruct((rows, 256), jnp.float32),
        in_specs=[SMEM] + [VMEM] * (1 + len(payloads) + len(olds)),
        out_specs=VMEM,
        input_output_aliases={2 + len(payloads): 0} if olds else {},
        scratch_shapes=[
            pltpu.VMEM((pairs, rows // 32, 128), jnp.int32),
            pltpu.VMEM((pairs, SLOTS, 128), jnp.int32),
            pltpu.VMEM((pairs, SLOTS, 128), jnp.int32),
        ],
        compiler_params=pltpu.CompilerParams(vmem_limit_bytes=GRANT * 1024 * 1024),
        cost_estimate=pl.CostEstimate(
            flops=4 * work * 256, bytes_accessed=1 << 22, transcendentals=work
        ),
    )(where, factors, *payloads, *olds)


def swap(value, axis, bit):
    size = lax.axis_size(axis)
    return lax.ppermute(value, axis, [(i, i ^ bit) for i in range(size)])


def shift_by(value, axis, step, inner=1):
    size = lax.axis_size(axis)
    return lax.ppermute(value, axis, [(i, (i + step * inner) % size) for i in range(size)])


def turn(value, step):
    size = lax.axis_size("label")
    return lax.ppermute(
        value, "label", [(i, (i + (2 - 4 * (i % 2)) * step) % size) for i in range(size)]
    )


def body(queries, basis, factors, positives, counts, placement):
    label, dp, part = lax.axis_index("label"), lax.axis_index("dp"), lax.axis_index("basis")
    block = factors.shape[0] // lax.axis_size("dp")
    half = (dp & 1) * OWN
    mine = lax.dynamic_slice_in_dim(factors, dp * block, block, 0)
    partial_value = lax.dot_general(
        queries, basis, (((1,), (1,)), ((), ())), preferred_element_type=jnp.float32
    )
    first_row = label * factors.shape[0] + dp * block
    where = jnp.stack([first_row, part * OWN, half]).astype(jnp.int32)
    digits = pl.pallas_call(
        digits_kernel,
        out_shape=jax.ShapeDtypeStruct((EXTRA, 256), jnp.bfloat16),
        in_specs=[SMEM, VMEM, VMEM, VMEM],
        out_specs=VMEM,
        cost_estimate=pl.CostEstimate(
            flops=1 << 31, bytes_accessed=1 << 19, transcendentals=0
        ),
    )(
        where,
        positives.T,
        counts.reshape(1, -1),
        placement.reshape(-1, 128),
    )

    def piece_of(value, step):
        count = value.shape[0] // lax.axis_size("basis")
        return lax.dynamic_slice_in_dim(value, ((part + step) & 3) * count, count, 0)

    rows = piece_of(partial_value, 0)
    moved = [shift_by(piece_of(partial_value, step), "basis", step) for step in (2, 1, 3)]
    for value in moved:
        rows = rows + value
    own = jnp.concatenate([rows.astype(jnp.bfloat16), digits], axis=0)
    next_own = swap(own, "dp", 1)
    even = dp & 1 == 0
    pair = jnp.concatenate(
        [
            jnp.where(even, own[:OWN], next_own[:OWN]),
            jnp.where(even, next_own[:OWN], own[:OWN]),
            own[OWN:] + next_own[OWN:],
        ],
        axis=0,
    )[None]
    others = [shift_by(pair, "dp", step) for step in (2, 6, 4)]
    ring = jnp.concatenate([pair] + others, axis=0)

    near = [turn(ring, 1), turn(ring, -1)]
    ring_other = swap(ring, "label", 1)
    far = turn(near[0], 1)
    near_other = [swap(value, "label", 1) for value in near]
    far_other = swap(far, "label", 1)
    sums = add_grads(where, mine, [ring])
    sums = add_grads(where, mine, [ring_other], sums)
    sums = add_grads(where, mine, near, sums)
    sums = add_grads(where, mine, near_other, sums)
    sums = add_grads(where, mine, [far, far_other], sums)

    order = (2, 1, 3)
    quarters = [piece_of(sums, step) for step in (0,) + order]
    total, *sent = lax.optimization_barrier(
        (quarters[0], *((value * SCALE).astype(LINK) for value in quarters[1:]))
    )
    total = total * SCALE
    for i, step in enumerate(order):
        total = total + shift_by(sent[i], "basis", step).astype(jnp.float32)
        if i == 0:
            total = lax.optimization_barrier(total)
    return total


def solution(mesh):
    placed = (
        P(("label", "dp"), "basis"),
        P(None, "basis"),
        P("label", None),
        P(("label", "dp"), None),
        P(("label", "dp")),
        P(),
    )
    return jax.shard_map(
        body,
        mesh=mesh,
        in_specs=placed,
        out_specs=P(("label", "dp", "basis"), None),
        check_vma=False,
    )
```

```python
import functools

import jax
import jax.numpy as jnp
from jax import lax
from jax.experimental import pallas as pl
from jax.experimental.pallas import tpu as pltpu
from jax.sharding import PartitionSpec as P


SLOTS = 16
OWN = 64
EXTRA = 16
PAIR = 2 * OWN
MIDDLE = 192
SCALE = 1.0 / 256.0
GRANT = 8
LINK = jnp.float16
NOWHERE = -250.0


def digits_kernel(pos_in, counts_in, place_in, out_ref, pos_ref, counts_ref, place_ref, sem):
    pairs = ((place_in, place_ref), (pos_in, pos_ref), (counts_in, counts_ref))
    copies = [pltpu.make_async_copy(a, b, sem.at[i]) for i, (a, b) in enumerate(pairs)]
    for copy in copies:
        copy.start()
    for copy in copies:
        copy.wait()
    start, half = lax.axis_index("basis") * OWN, (lax.axis_index("dp") & 1) * OWN
    table = place_ref[...]
    high = ((table >> 8) - MIDDLE).astype(jnp.float32).astype(jnp.bfloat16)
    low = (table & 255).astype(jnp.float32).astype(jnp.bfloat16)
    tables = jnp.concatenate([high, low], axis=1)
    count = SLOTS // 2
    lane = lax.broadcasted_iota(jnp.int32, (count, 128), 1)
    lower = lane < OWN
    early = pltpu.roll(pos_ref[:count, :], (256 - start) & 255, 1)[:, :128]
    late = pltpu.roll(pos_ref[count:, :], (256 + OWN - start) & 255, 1)[:, :128]
    pos = jnp.where(lower, early, late)
    groups = table.shape[0]
    row = lax.broadcasted_iota(jnp.int32, (groups, 256), 0)
    spot = lax.broadcasted_iota(jnp.int32, (128, 256), 0)
    firsts, seconds = [], []
    for k in range(count // 2):
        one = jnp.concatenate([pos[2 * k : 2 * k + 1, :], pos[2 * k + 1 : 2 * k + 2, :]], axis=1)
        hot = jnp.where(row == (one >> 7), 1.0, 0.0).astype(jnp.bfloat16)
        both = lax.dot_general(tables, hot, (((0,), (0,)), ((), ())), preferred_element_type=jnp.float32)
        pick = spot == (one & 127)
        first = jnp.sum(jnp.where(pick, both[:128], 0.0), axis=0, keepdims=True)
        second = jnp.sum(jnp.where(pick, both[128:], 0.0), axis=0, keepdims=True)
        firsts += [first[:, :128], first[:, 128:]]
        seconds += [second[:, :128], second[:, 128:]]
    first = jnp.concatenate(firsts, axis=0)
    second = jnp.concatenate(seconds, axis=0)
    counts = jnp.broadcast_to(counts_ref[...], (count, 256))
    counts = pltpu.roll(counts, (256 + half - start) & 255, 1)[:, :128]
    mine = (lane >= half) & (lane < half + OWN)
    slot = lax.broadcasted_iota(jnp.int32, (count, 128), 0)

    def placed(value, shift, used, nothing):
        return jnp.where(mine, jnp.where(used, pltpu.roll(value, shift, 1), nothing), 0.0)

    highs, lows = [], []
    for shift, base in ((half, 0), (OWN - half, count)):
        used = slot + base < counts
        highs.append(placed(first, shift, used, NOWHERE))
        lows.append(placed(second, shift, used, 0.0))
    out_ref[...] = jnp.concatenate(
        [jnp.concatenate(highs, axis=0), jnp.concatenate(lows, axis=0)], axis=1
    ).astype(jnp.bfloat16)


def build_words(base, payload_refs, words_ref, word_ref, bit_ref):
    spot = 0
    for payload_ref in payload_refs:
        for p in range(payload_ref.shape[0]):
            both = payload_ref[p, PAIR:, :].astype(jnp.float32).astype(jnp.int32)
            local = (both[:, :128] + MIDDLE) * 256 + both[:, 128:] - base
            word_ref[spot] = local >> 5
            bit_ref[spot] = jnp.left_shift(1, local & 31)
            spot += 1
    shape = words_ref.shape[1:]
    order = lax.broadcasted_iota(jnp.int32, shape, 0)

    def build(p, carry):
        found = jnp.zeros(shape, jnp.int32)
        for k in range(SLOTS):
            word = jnp.broadcast_to(word_ref[p, k : k + 1, :], shape)
            bit = jnp.broadcast_to(bit_ref[p, k : k + 1, :], shape)
            found = found | jnp.where(order == word, bit, 0)
        words_ref[p] = found
        return carry

    lax.fori_loop(0, spot, build, 0)


def block_grads(factor_ref, payload_refs, words_ref):
    word_count = words_ref.shape[1]
    bits = jnp.left_shift(1, lax.broadcasted_iota(jnp.int32, (32, 128), 0))
    proj = [ref[:, :PAIR, :].reshape(-1, 256) for ref in payload_refs]
    proj = proj[0] if len(proj) == 1 else jnp.concatenate(proj, axis=0)
    scores = lax.dot_general(
        factor_ref[...],
        proj * jnp.bfloat16(0.5),
        (((1,), (1,)), ((), ())),
        preferred_element_type=jnp.float32,
    )
    tanh = jnp.tanh(scores)
    columns = []
    for c in range(proj.shape[0] // 128):
        found = words_ref[c]
        rows = []
        for m in range(word_count):
            hit = (jnp.broadcast_to(found[m : m + 1, :], (32, 128)) & bits) != 0
            piece = tanh[m * 32 : m * 32 + 32, c * 128 : c * 128 + 128]
            rows.append((piece + jnp.where(hit, -1.0, 1.0)).astype(jnp.bfloat16))
        columns.append(jnp.concatenate(rows, axis=0))
    grad = jnp.concatenate(columns, axis=1)
    return jnp.dot(grad, proj, preferred_element_type=jnp.float32)


def grads_kernel(payloads, adds, factor_ref, *refs):
    payload_refs, refs = refs[:payloads], refs[payloads:]
    olds, (out_ref, words_ref, word_ref, bit_ref) = refs[:adds], refs[adds:]
    place = lax.axis_index("label") * lax.axis_size("dp") + lax.axis_index("dp")
    base = place * factor_ref.shape[0]
    build_words(base, payload_refs, words_ref, word_ref, bit_ref)
    value = block_grads(factor_ref, payload_refs, words_ref)
    out_ref[...] = olds[0][...] + value if adds else value


VMEM = pl.BlockSpec(memory_space=pltpu.VMEM)
ANY = pl.BlockSpec(memory_space=pl.ANY)


def add_grads(factors, payloads, *olds):
    rows = factors.shape[0]
    pairs = sum(payload.shape[0] for payload in payloads)
    work = rows * pairs * PAIR
    return pl.pallas_call(
        functools.partial(grads_kernel, len(payloads), len(olds)),
        out_shape=jax.ShapeDtypeStruct((rows, 256), jnp.float32),
        in_specs=[VMEM] * (1 + len(payloads) + len(olds)),
        out_specs=VMEM,
        scratch_shapes=[
            pltpu.VMEM((pairs, rows // 32, 128), jnp.int32),
            pltpu.VMEM((pairs, SLOTS, 128), jnp.int32),
            pltpu.VMEM((pairs, SLOTS, 128), jnp.int32),
        ],
        compiler_params=pltpu.CompilerParams(vmem_limit_bytes=GRANT * 1024 * 1024),
        cost_estimate=pl.CostEstimate(
            flops=4 * work * 256, bytes_accessed=1 << 22, transcendentals=work
        ),
    )(factors, *payloads, *olds)


def swap(value, axis, bit):
    size = lax.axis_size(axis)
    return lax.ppermute(value, axis, [(i, i ^ bit) for i in range(size)])


def shift_by(value, axis, step, inner=1):
    size = lax.axis_size(axis)
    return lax.ppermute(value, axis, [(i, (i + step * inner) % size) for i in range(size)])


def turn(value, step):
    size = lax.axis_size("label")
    return lax.ppermute(
        value, "label", [(i, (i + (2 - 4 * (i % 2)) * step) % size) for i in range(size)]
    )


def body(queries, basis, factors, positives, counts, placement):
    dp, part = lax.axis_index("dp"), lax.axis_index("basis")
    block = factors.shape[0] // lax.axis_size("dp")
    mine = lax.dynamic_slice_in_dim(factors, dp * block, block, 0)
    partial_value = lax.dot_general(
        queries, basis, (((1,), (1,)), ((), ())), preferred_element_type=jnp.float32
    )
    digits = pl.pallas_call(
        digits_kernel,
        out_shape=jax.ShapeDtypeStruct((EXTRA, 256), jnp.bfloat16),
        in_specs=[ANY, ANY, ANY],
        out_specs=VMEM,
        scratch_shapes=[
            pltpu.VMEM(positives.shape[::-1], jnp.int32),
            pltpu.VMEM((1, counts.shape[0]), jnp.int32),
            pltpu.VMEM((placement.shape[0] // 128, 128), jnp.int32),
            pltpu.SemaphoreType.DMA((3,)),
        ],
        cost_estimate=pl.CostEstimate(
            flops=1 << 31, bytes_accessed=1 << 19, transcendentals=0
        ),
    )(
        positives.T,
        counts.reshape(1, -1),
        placement.reshape(-1, 128),
    )

    def piece_of(value, step):
        count = value.shape[0] // lax.axis_size("basis")
        return lax.dynamic_slice_in_dim(value, ((part + step) & 3) * count, count, 0)

    rows = piece_of(partial_value, 0)
    moved = [shift_by(piece_of(partial_value, step), "basis", step) for step in (2, 1, 3)]
    for value in moved:
        rows = rows + value
    own = lax.optimization_barrier(jnp.concatenate([rows.astype(jnp.bfloat16), digits], axis=0))
    next_own = swap(own, "dp", 1)
    even = dp & 1 == 0
    pair = jnp.concatenate(
        [
            jnp.where(even, own[:OWN], next_own[:OWN]),
            jnp.where(even, next_own[:OWN], own[:OWN]),
            own[OWN:] + next_own[OWN:],
        ],
        axis=0,
    )[None]
    others = [shift_by(pair, "dp", step) for step in (2, 6, 4)]
    ring = jnp.concatenate([pair] + others, axis=0)

    near = [turn(ring, 1)]
    near.append(turn(ring, -1))
    ring_other = swap(ring, "label", 1)
    far = turn(near[0], 1)
    near_other = [swap(value, "label", 1) for value in near]
    far_other = swap(far, "label", 1)
    sums = add_grads(mine, [ring])
    sums = add_grads(mine, [ring_other], sums)
    sums = add_grads(mine, near, sums)
    sums = add_grads(mine, near_other, sums)
    sums = add_grads(mine, [far, far_other], sums)

    order = (2, 1, 3)
    quarters = [piece_of(sums, step) for step in (0,) + order]
    total, *sent = lax.optimization_barrier(
        (quarters[0], *((value * SCALE).astype(LINK) for value in quarters[1:]))
    )
    total = total * SCALE
    for i, step in enumerate(order):
        total = total + shift_by(sent[i], "basis", step).astype(jnp.float32)
        if i == 0:
            total = lax.optimization_barrier(total)
    return total


def solution(mesh):
    placed = (
        P(("label", "dp"), "basis"),
        P(None, "basis"),
        P("label", None),
        P(("label", "dp"), None),
        P(("label", "dp")),
        P(),
    )
    return jax.shard_map(
        body,
        mesh=mesh,
        in_specs=placed,
        out_specs=P(("label", "dp", "basis"), None),
        check_vma=False,
    )
```

```python
import functools

import jax
import jax.numpy as jnp
from jax import lax
from jax.experimental import pallas as pl
from jax.experimental.pallas import tpu as pltpu
from jax.sharding import PartitionSpec as P


SLOTS = 16
OWN = 64
EXTRA = 16
PAIR = 2 * OWN
MIDDLE = 192
SCALE = 1.0 / 256.0
GRANT = 8
LINK = jnp.float16
NOWHERE = -250.0


def digits_kernel(pos_in, counts_in, place_in, out_ref, pos_ref, counts_ref, place_ref, sem):
    pairs = ((place_in, place_ref), (pos_in, pos_ref), (counts_in, counts_ref))
    copies = [pltpu.make_async_copy(a, b, sem.at[i]) for i, (a, b) in enumerate(pairs)]
    for copy in copies:
        copy.start()
    for copy in copies:
        copy.wait()
    start, half = lax.axis_index("basis") * OWN, (lax.axis_index("dp") & 1) * OWN
    table = place_ref[...]
    high = ((table >> 8) - MIDDLE).astype(jnp.float32).astype(jnp.bfloat16)
    low = (table & 255).astype(jnp.float32).astype(jnp.bfloat16)
    tables = jnp.concatenate([high, low], axis=1)
    count = SLOTS // 2
    lane = lax.broadcasted_iota(jnp.int32, (count, 128), 1)
    lower = lane < OWN
    early = pltpu.roll(pos_ref[:count, :], (256 - start) & 255, 1)[:, :128]
    late = pltpu.roll(pos_ref[count:, :], (256 + OWN - start) & 255, 1)[:, :128]
    pos = jnp.where(lower, early, late)
    groups = table.shape[0]
    row = lax.broadcasted_iota(jnp.int32, (groups, 256), 0)
    spot = lax.broadcasted_iota(jnp.int32, (128, 256), 0)
    firsts, seconds = [], []
    for k in range(count // 2):
        one = jnp.concatenate([pos[2 * k : 2 * k + 1, :], pos[2 * k + 1 : 2 * k + 2, :]], axis=1)
        hot = jnp.where(row == (one >> 7), 1.0, 0.0).astype(jnp.bfloat16)
        both = lax.dot_general(tables, hot, (((0,), (0,)), ((), ())), preferred_element_type=jnp.float32)
        pick = spot == (one & 127)
        first = jnp.sum(jnp.where(pick, both[:128], 0.0), axis=0, keepdims=True)
        second = jnp.sum(jnp.where(pick, both[128:], 0.0), axis=0, keepdims=True)
        firsts += [first[:, :128], first[:, 128:]]
        seconds += [second[:, :128], second[:, 128:]]
    first = jnp.concatenate(firsts, axis=0)
    second = jnp.concatenate(seconds, axis=0)
    counts = jnp.broadcast_to(counts_ref[...], (count, 256))
    counts = pltpu.roll(counts, (256 + half - start) & 255, 1)[:, :128]
    mine = (lane >= half) & (lane < half + OWN)
    slot = lax.broadcasted_iota(jnp.int32, (count, 128), 0)

    def placed(value, shift, used, nothing):
        return jnp.where(mine, jnp.where(used, pltpu.roll(value, shift, 1), nothing), 0.0)

    highs, lows = [], []
    for shift, base in ((half, 0), (OWN - half, count)):
        used = slot + base < counts
        highs.append(placed(first, shift, used, NOWHERE))
        lows.append(placed(second, shift, used, 0.0))
    out_ref[...] = jnp.concatenate(
        [jnp.concatenate(highs, axis=0), jnp.concatenate(lows, axis=0)], axis=1
    ).astype(jnp.bfloat16)


def build_words(base, payload_refs, words_ref, word_ref, bit_ref):
    spot = 0
    for payload_ref in payload_refs:
        for p in range(payload_ref.shape[0]):
            both = payload_ref[p, PAIR:, :].astype(jnp.float32).astype(jnp.int32)
            local = (both[:, :128] + MIDDLE) * 256 + both[:, 128:] - base
            word_ref[spot] = local >> 5
            bit_ref[spot] = jnp.left_shift(1, local & 31)
            spot += 1
    shape = words_ref.shape[1:]
    order = lax.broadcasted_iota(jnp.int32, shape, 0)

    def build(p, carry):
        found = jnp.zeros(shape, jnp.int32)
        for k in range(SLOTS):
            word = jnp.broadcast_to(word_ref[p, k : k + 1, :], shape)
            bit = jnp.broadcast_to(bit_ref[p, k : k + 1, :], shape)
            found = found | jnp.where(order == word, bit, 0)
        words_ref[p] = found
        return carry

    lax.fori_loop(0, spot, build, 0)


def block_grads(factor_ref, payload_refs, words_ref):
    word_count = words_ref.shape[1]
    bits = jnp.left_shift(1, lax.broadcasted_iota(jnp.int32, (32, 128), 0))
    proj = [ref[:, :PAIR, :].reshape(-1, 256) for ref in payload_refs]
    proj = proj[0] if len(proj) == 1 else jnp.concatenate(proj, axis=0)
    scores = lax.dot_general(
        factor_ref[...],
        proj * jnp.bfloat16(0.5),
        (((1,), (1,)), ((), ())),
        preferred_element_type=jnp.float32,
    )
    tanh = jnp.tanh(scores)
    columns = []
    for c in range(proj.shape[0] // 128):
        found = words_ref[c]
        rows = []
        for m in range(word_count):
            hit = (jnp.broadcast_to(found[m : m + 1, :], (32, 128)) & bits) != 0
            piece = tanh[m * 32 : m * 32 + 32, c * 128 : c * 128 + 128]
            rows.append((piece + jnp.where(hit, -1.0, 1.0)).astype(jnp.bfloat16))
        columns.append(jnp.concatenate(rows, axis=0))
    grad = jnp.concatenate(columns, axis=1)
    return jnp.dot(grad, proj, preferred_element_type=jnp.float32)


def grads_kernel(payloads, adds, factor_ref, *refs):
    payload_refs, refs = refs[:payloads], refs[payloads:]
    olds, (out_ref, words_ref, word_ref, bit_ref) = refs[:adds], refs[adds:]
    place = lax.axis_index("label") * lax.axis_size("dp") + lax.axis_index("dp")
    base = place * factor_ref.shape[0]
    build_words(base, payload_refs, words_ref, word_ref, bit_ref)
    value = block_grads(factor_ref, payload_refs, words_ref)
    out_ref[...] = olds[0][...] + value if adds else value


VMEM = pl.BlockSpec(memory_space=pltpu.VMEM)
ANY = pl.BlockSpec(memory_space=pl.ANY)


def add_grads(factors, payloads, *olds):
    rows = factors.shape[0]
    pairs = sum(payload.shape[0] for payload in payloads)
    work = rows * pairs * PAIR
    return pl.pallas_call(
        functools.partial(grads_kernel, len(payloads), len(olds)),
        out_shape=jax.ShapeDtypeStruct((rows, 256), jnp.float32),
        in_specs=[VMEM] * (1 + len(payloads) + len(olds)),
        out_specs=VMEM,
        scratch_shapes=[
            pltpu.VMEM((pairs, rows // 32, 128), jnp.int32),
            pltpu.VMEM((pairs, SLOTS, 128), jnp.int32),
            pltpu.VMEM((pairs, SLOTS, 128), jnp.int32),
        ],
        compiler_params=pltpu.CompilerParams(vmem_limit_bytes=GRANT * 1024 * 1024),
        cost_estimate=pl.CostEstimate(
            flops=4 * work * 256, bytes_accessed=1 << 22, transcendentals=work
        ),
    )(factors, *payloads, *olds)


def swap(value, axis, bit):
    size = lax.axis_size(axis)
    return lax.ppermute(value, axis, [(i, i ^ bit) for i in range(size)])


def shift_by(value, axis, step, inner=1):
    size = lax.axis_size(axis)
    return lax.ppermute(value, axis, [(i, (i + step * inner) % size) for i in range(size)])


def turn(value, step):
    size = lax.axis_size("label")
    return lax.ppermute(
        value, "label", [(i, (i + (2 - 4 * (i % 2)) * step) % size) for i in range(size)]
    )


def body(queries, basis, factors, positives, counts, placement):
    dp, part = lax.axis_index("dp"), lax.axis_index("basis")
    block = factors.shape[0] // lax.axis_size("dp")
    mine = lax.dynamic_slice_in_dim(factors, dp * block, block, 0)
    partial_value = lax.dot_general(
        queries, basis, (((1,), (1,)), ((), ())), preferred_element_type=jnp.float32
    )
    digits = pl.pallas_call(
        digits_kernel,
        out_shape=jax.ShapeDtypeStruct((EXTRA, 256), jnp.bfloat16),
        in_specs=[ANY, ANY, ANY],
        out_specs=VMEM,
        scratch_shapes=[
            pltpu.VMEM(positives.shape[::-1], jnp.int32),
            pltpu.VMEM((1, counts.shape[0]), jnp.int32),
            pltpu.VMEM((placement.shape[0] // 128, 128), jnp.int32),
            pltpu.SemaphoreType.DMA((3,)),
        ],
        cost_estimate=pl.CostEstimate(
            flops=1 << 31, bytes_accessed=1 << 19, transcendentals=0
        ),
    )(
        positives.T,
        counts.reshape(1, -1),
        placement.reshape(-1, 128),
    )

    def piece_of(value, step):
        count = value.shape[0] // lax.axis_size("basis")
        return lax.dynamic_slice_in_dim(value, ((part + step) & 3) * count, count, 0)

    rows = piece_of(partial_value, 0)
    moved = [shift_by(piece_of(partial_value, step), "basis", step) for step in (2, 1, 3)]
    for value in moved:
        rows = rows + value
    own = lax.optimization_barrier(jnp.concatenate([rows.astype(jnp.bfloat16), digits], axis=0))
    next_own = swap(own, "dp", 1)
    even = dp & 1 == 0
    pair = jnp.concatenate(
        [
            jnp.where(even, own[:OWN], next_own[:OWN]),
            jnp.where(even, next_own[:OWN], own[:OWN]),
            own[OWN:] + next_own[OWN:],
        ],
        axis=0,
    )[None]
    others = [shift_by(pair, "dp", step) for step in (2, 6, 4)]
    ring = jnp.concatenate([pair] + others, axis=0)

    near = [turn(ring, 1)]
    near.append(turn(ring, -1))
    ring_other = swap(ring, "label", 1)
    far = turn(near[0], 1)
    near_other = [swap(value, "label", 1) for value in near]
    far_other = swap(far, "label", 1)
    sums = add_grads(mine, [ring])
    sums = add_grads(mine, [ring_other], sums)
    sums = add_grads(mine, near, sums)
    later = add_grads(mine, near_other)
    later = add_grads(mine, [far, far_other], later)

    order = (2, 1, 3)
    quarters = [piece_of(sums, step) + piece_of(later, step) for step in (0,) + order]
    total, *sent = lax.optimization_barrier(
        (quarters[0], *((value * SCALE).astype(LINK) for value in quarters[1:]))
    )
    total = total * SCALE
    for i, step in enumerate(order):
        total = total + shift_by(sent[i], "basis", step).astype(jnp.float32)
        if i == 0:
            total = lax.optimization_barrier(total)
    return total


def solution(mesh):
    placed = (
        P(("label", "dp"), "basis"),
        P(None, "basis"),
        P("label", None),
        P(("label", "dp"), None),
        P(("label", "dp")),
        P(),
    )
    return jax.shard_map(
        body,
        mesh=mesh,
        in_specs=placed,
        out_specs=P(("label", "dp", "basis"), None),
        check_vma=False,
    )
```
